256 devices in a mesh: exp: 32 (over z_hi, y, core), et: 8 (over z_lo, x).
Axes of the slice: x: 4, y: 4, z: 8 (z_hi: 4, z_lo: 2; z = z_hi * 2 + z_lo), core: 2. Of those that a mesh axis runs over, the one named last changes fastest.
Arguments:
- tokens: bfloat16 [1536, 7168], P(('exp', 'et')), may hold values from -6 to 6
- grad_out: bfloat16 [1536, 7168], P(('exp', 'et')), may hold values from -6 to 6
- gates: bfloat16 [1536, 8], P(('exp', 'et')), may hold values from 0.049804688 to 1
- expert_ids: int32 [1536, 8], P(('exp', 'et')), may hold values from 0 to 31, all different within a row; in each aligned block of 6 rows (0 to 5, 6 to 11, ...) at most 2 rows name the same one
- gate_weight: bfloat16 [32, 7168, 1024], P('exp', None, 'et'), may hold values from -0.0625 to 0.0625
- up_weight: bfloat16 [32, 7168, 1024], P('exp', None, 'et'), may hold values from -0.0625 to 0.0625
- down_weight: bfloat16 [32, 1024, 7168], P('exp', 'et'), may hold values from -0.1875 to 0.1875
Outputs:
- input_grad: bfloat16 [1536, 7168], P(('exp', 'et'))
- gate_grad: float32 [1536, 8], P(('exp', 'et'))
- gate_weight_grad: bfloat16 [32, 7168, 1024], P('exp', None, 'et')
- up_weight_grad: bfloat16 [32, 7168, 1024], P('exp', None, 'et')
- down_weight_grad: bfloat16 [32, 1024, 7168], P('exp', 'et')
The draws below stay inside these ranges and needn't reach their ends.
Inputs may be any that keep to these rules, and one draw needn't show every extreme that they name: `expert_ids`: each row names 8 different experts. Among the 6 tokens of one device no expert is named by more than 2 tokens, and in every draw some expert is named by exactly 2 tokens of some device.
All inputs are finite; a program needn't handle non-finite values.
Results may differ from the reference program's by a relative error of at most 0.017.
Values may be sent and summed in bfloat16 or wider, within the bound.
A program may use at most 128 MiB of HBM per device.

```python
import math
import jax
import jax.numpy as jnp
import numpy as np
from jax import lax

D = 7168
TOP = 8
FF = 1024
TOK_DEV = 6
EXPERTS = 32
TOKENS = 1536
CAP = 2
N_ET = 8


def level_of(stream_key, extent, pieces, low, top_value):
    loudness, own = 1.0, jax.random.fold_in(stream_key, 6)
    for position, parts in pieces:
        heights = jnp.exp(jax.random.uniform(jax.random.fold_in(own, position), (parts,), jnp.float32, low / len(pieces), top_value / len(pieces)))
        loudness = loudness * jnp.repeat(heights, extent[position] // parts).reshape([-1 if axis == position else 1 for axis in range(len(extent))])
    return loudness


def assign_block(key, own, number, rows, number_of, top, reach, lean):
    sequence = jax.random.permutation(key, number_of)
    packed, common = portions_of(number_of, rows * top, reach, lean, True), portions_of(number_of, rows * top, reach, lean, False)
    places = jnp.arange(number_of)

    def named(lengths, offset_by):
        used = int((lengths > 0).sum())
        fixed = max(1, used // 4)
        moved = fixed + (places - fixed + offset_by * (used - fixed)) % max(1, number_of - fixed)
        return jnp.zeros((number_of,), jnp.int32).at[sequence[jnp.where(places < fixed, places, moved)]].set(jnp.asarray(lengths, jnp.int32))

    lengths = jnp.where(number % 4 == 0, named(packed, number // 4), named(common, number - number // 4 - 1))
    mixed = jax.random.permutation(jax.random.fold_in(own, 3), number_of)
    giver, taker = mixed[0:number_of // 2 * 2:2], mixed[1:number_of // 2 * 2:2]
    slack = jnp.minimum(lengths[giver] - 1, reach - lengths[taker]) // 2
    slack = jnp.where((giver == sequence[0]) | (taker == sequence[0]) | (lengths[taker] == 0), 0, jnp.maximum(slack, 0))
    moved = jax.random.randint(jax.random.fold_in(own, 4), (number_of // 2,), 0, 1 << 20) % (slack + 1)
    lengths = lengths.at[giver].add(-moved).at[taker].add(moved)
    members = jnp.searchsorted(jnp.cumsum(lengths), jnp.arange(rows * top), side="right").astype(jnp.int32)
    listing = members.reshape(top, rows).T
    listing = listing[jax.random.permutation(jax.random.fold_in(own, 1), rows)]
    offset_by = jax.random.randint(jax.random.fold_in(own, 2), (rows, 1), 0, top)
    return jnp.take_along_axis(listing, (jnp.arange(top)[None, :] + offset_by) % top, axis=1)


def portions_of(amount, total, most, lean, full):
    portions = [(1 << 20) // math.isqrt(rank ** lean) + 1 for rank in range(1, amount + 1)]
    largest = most if full else min(most, max(-(-total // amount), total * portions[0] // sum(portions)))
    least = 1 if total - largest >= amount - 1 else 0
    given, rest = [largest] + [least] * (amount - 1), total - largest - least * (amount - 1)
    while rest > 0:
        free = [i for i in range(1, amount) if given[i] < largest] or [i for i in range(1, amount) if given[i] < most]
        whole, budget = sum([portions[i] for i in free]), rest
        for i in free:
            addition = min(most - given[i], max(1, budget * portions[i] // whole), rest)
            given[i] = given[i] + addition
            rest = rest - addition
    return np.array(given)


def centred(own_key, extent, width, most, shards=(), kind=jnp.bfloat16):
    entries = jax.random.normal(own_key, extent, jnp.float32) * width
    if len(shards) > 0:
        entries = level_of(own_key, extent, shards, -0.22, 0.18) * entries
    return jnp.clip(entries, min=-most, max=most).astype(kind)


def setup_inputs(seed: int = 0) -> dict:
    splits = jax.random.split(jax.random.key(seed), 8)
    tokens = centred(splits[0], (TOKENS, D), 1.0, 6.0, ((0, 256),))
    grad_out = centred(splits[1], (TOKENS, D), 1.0, 6.0, ((0, 256),))
    gates = jnp.clip(jnp.exp(math.log(1.0) - 2.9996462 * jax.random.uniform(splits[2], (TOKENS, TOP), jnp.float32) ** level_of(splits[2], (TOKENS, TOP), ((0, 256),), -0.2, 0.2)), 0.049804688, 1.0).astype(jnp.bfloat16)
    expert_ids_keys = jax.random.split(jax.random.fold_in(splits[3], 1), TOKENS // TOK_DEV)
    expert_ids_turns = jax.random.permutation(jax.random.fold_in(splits[3], 3), TOKENS // TOK_DEV)
    expert_ids = jax.vmap(lambda own, number: assign_block(jax.random.fold_in(splits[3], 2), own, number, TOK_DEV, EXPERTS, TOP, CAP, 2))(expert_ids_keys, expert_ids_turns).reshape((TOKENS, TOP))
    gate_weight = centred(splits[4], (EXPERTS, D, FF), D ** -0.5, 0.0625, ((0, 32), (2, 8)))
    up_weight = centred(splits[5], (EXPERTS, D, FF), D ** -0.5, 0.0625, ((0, 32), (2, 8)))
    down_weight = centred(splits[6], (EXPERTS, FF, D), FF ** -0.5, 0.1875, ((0, 32), (1, 8)))
    return {"tokens": tokens, "grad_out": grad_out, "gates": gates, "expert_ids": expert_ids, "gate_weight": gate_weight, "up_weight": up_weight, "down_weight": down_weight}


def expert_terms(rows_x, rows_dy, rows_g, w_gate, w_up, w_down):
    gate_pre = jnp.dot(rows_x, w_gate, preferred_element_type=jnp.float32)
    up_pre = jnp.dot(rows_x, w_up, preferred_element_type=jnp.float32)
    sigma = jax.nn.sigmoid(gate_pre)
    silu_val = gate_pre * sigma
    act = silu_val * up_pre
    back = lax.dot_general(rows_dy, w_down, (((1,), (1,)), ((), ())), preferred_element_type=jnp.float32)
    product = act * back
    scale = rows_g.astype(jnp.float32)[:, None]
    weighted = (scale * act).astype(jnp.bfloat16)
    dact = scale * back
    grad_gate = (dact * up_pre * sigma * (1.0 + gate_pre * (1.0 - sigma))).astype(jnp.bfloat16)
    grad_up = (dact * silu_val).astype(jnp.bfloat16)
    share = w_gate.shape[1] // N_ET
    inward = jnp.zeros((rows_x.shape[0], rows_x.shape[1]), jnp.float32)
    score = jnp.zeros((rows_x.shape[0],), jnp.float32)
    for index in range(N_ET):
        low = index * share
        high = low + share
        piece = lax.dot_general(grad_gate[:, low:high], w_gate[:, low:high], (((1,), (1,)), ((), ())), preferred_element_type=jnp.float32)
        piece = piece + lax.dot_general(grad_up[:, low:high], w_up[:, low:high], (((1,), (1,)), ((), ())), preferred_element_type=jnp.float32)
        inward = inward + lax.optimization_barrier(piece.astype(jnp.bfloat16)).astype(jnp.float32)
        part_score = jnp.sum(product[:, low:high], axis=1)
        score = score + lax.optimization_barrier(part_score.astype(jnp.bfloat16)).astype(jnp.float32)
    d_gate = lax.dot_general(rows_x, grad_gate, (((0,), (0,)), ((), ())), preferred_element_type=jnp.float32)
    d_up = lax.dot_general(rows_x, grad_up, (((0,), (0,)), ((), ())), preferred_element_type=jnp.float32)
    d_down = lax.dot_general(weighted, rows_dy, (((0,), (0,)), ((), ())), preferred_element_type=jnp.float32)
    return d_gate, d_up, d_down, inward, score


def reference(tokens, grad_out, gates, expert_ids, gate_weight, up_weight, down_weight):
    count = tokens.shape[0]
    depth = tokens.shape[1]
    pairs = count * TOP
    flat = expert_ids.reshape(-1).astype(jnp.int32)
    onehot = (flat[:, None] == jnp.arange(EXPERTS, dtype=jnp.int32)[None, :]).astype(jnp.int32)
    rank = jnp.sum((jnp.cumsum(onehot, axis=0) - onehot) * onehot, axis=1)
    limit = (count // TOK_DEV) * CAP
    slots = flat * limit + rank
    table = jnp.full((EXPERTS * limit,), pairs, jnp.int32).at[slots].set(jnp.arange(pairs, dtype=jnp.int32))
    table = table.reshape(EXPERTS, limit)
    x_pad = jnp.concatenate([tokens, jnp.zeros((1, depth), tokens.dtype)], axis=0)
    dy_pad = jnp.concatenate([grad_out, jnp.zeros((1, depth), grad_out.dtype)], axis=0)
    g_pad = jnp.concatenate([gates.reshape(-1), jnp.zeros((1,), gates.dtype)], axis=0)

    def one_expert(carry, inputs):
        grad_acc, score_acc = carry
        w_gate, w_up, w_down, rows = inputs
        owner = (rows // TOP).astype(jnp.int32)
        terms = expert_terms(x_pad[owner], dy_pad[owner], g_pad[rows], w_gate, w_up, w_down)
        grad_acc = grad_acc.at[owner].add(terms[3])
        score_acc = score_acc.at[rows].set(terms[4])
        return (grad_acc, score_acc), (terms[0].astype(jnp.bfloat16), terms[1].astype(jnp.bfloat16), terms[2].astype(jnp.bfloat16))

    init = (jnp.zeros((count + 1, depth), jnp.float32), jnp.zeros((pairs + 1,), jnp.float32))
    (grad_acc, score_acc), (d_gate, d_up, d_down) = lax.scan(one_expert, init, (gate_weight, up_weight, down_weight, table))
    input_grad = grad_acc[:count].astype(jnp.bfloat16)
    gate_grad = score_acc[:pairs].reshape(count, TOP)
    return (input_grad, gate_grad, d_gate, d_up, d_down)
```

```python
import functools
import jax
import jax.numpy as jnp
from jax import lax
from jax.experimental import pallas as pl
from jax.experimental.pallas import tpu as pltpu
from jax.sharding import PartitionSpec as P

TOP = 8
LANE = 128
NS = 6
OCT = 8
MESH = pl.DeviceIdType.MESH
ORDERS = (("x", "y", "z"), ("y", "z", "x"), ("z", "x", "y"))
F32 = jnp.float32
BF16 = jnp.bfloat16


class Torus:
    def __init__(self, nx, ny, nzh, nzl):
        self.n = {"x": nx, "y": ny, "z": nzh * nzl}
        self.nzh, self.nzl = nzh, nzl

    def here(self):
        e = lax.axis_index("exp")
        t = lax.axis_index("et")
        ny, nx = self.n["y"], self.n["x"]
        core = lax.rem(e, 2)
        y = lax.rem(lax.div(e, 2), ny)
        zh = lax.div(e, 2 * ny)
        x = lax.rem(t, nx)
        zl = lax.div(t, nx)
        return {"x": x, "y": y, "z": zh * self.nzl + zl}, core

    def device(self, pos, core):
        zh = lax.div(pos["z"], self.nzl)
        zl = lax.rem(pos["z"], self.nzl)
        return {
            "exp": (zh * self.n["y"] + pos["y"]) * 2 + core,
            "et": zl * self.n["x"] + pos["x"],
        }

    def shift(self, pos, axis, by):
        n = self.n[axis]
        return lax.rem(pos[axis] + (by % n + n), n)

    def neighbour(self, pos, core, axis, by):
        other = dict(pos)
        other[axis] = self.shift(pos, axis, by)
        return self.device(other, core)

    def partners(self, pos, core):
        out = [self.device(pos, 1 - core)]
        for axis in "xyz":
            for d in (1, -1):
                out.append(self.neighbour(pos, core, axis, d))
        return out

    def steps(self, order):
        out = []
        for phase, axis in enumerate(order):
            for k in range(self.n[axis] - 1):
                out.append((phase, k))
        return out

    def weight(self, order, phase, reverse):
        w = 1
        done = order[phase + 1:] if reverse else order[:phase]
        for axis in done:
            w *= self.n[axis]
        return w

    def events(self, orders, reverse):
        out = []
        for s in range(NS):
            order = orders[s // 2]
            at = 0.0
            for i, (phase, k) in enumerate(self.steps(order)):
                at += self.weight(order, phase, reverse) + 0.3
                out.append((at, s, i))
        return [(s, i) for _, s, i in sorted(out)]


def greet(torus, pos, core):
    barrier = pltpu.get_barrier_semaphore()
    partners = torus.partners(pos, core)
    for p in partners:
        pl.semaphore_signal(barrier, inc=1, device_id=p, device_id_type=MESH)
    pl.semaphore_wait(barrier, len(partners))


def cut(torus, ref, width, core, s, at):
    if at.get("z") is None:
        zl, zh = slice(None), slice(None)
    else:
        zl, zh = lax.rem(at["z"], torus.nzl), lax.div(at["z"], torus.nzl)
    y = slice(None) if at.get("y") is None else at["y"]
    if at.get("x") is None:
        col = slice(None)
    else:
        col = pl.ds(pl.multiple_of(at["x"] * width, LANE), width)
    if core is None:
        return ref.at[zl, zh, y, s, :, col]
    return ref.at[zl, zh, y, core, s, :, col]


def gather_kernel(torus, width, blk, out, loc, send, recv, sib_send, sib_recv):
    pos, core = torus.here()
    sibling = torus.device(pos, 1 - core)
    greet(torus, pos, core)
    steps = [torus.steps(ORDERS[s // 2]) for s in range(NS)]

    def region(s, phase, shift):
        order = ORDERS[s // 2]
        at = dict(pos)
        for axis in order[:phase]:
            at[axis] = None
        at[order[phase]] = torus.shift(pos, order[phase], shift)
        return cut(torus, out, width, core, s, at)

    own = [cut(torus, out, width, core, s, pos) for s in range(NS)]

    def ring(s, i):
        phase, k = steps[s][i]
        d = 1 if s % 2 == 0 else -1
        dst = region(s, phase, -d * k)
        src = blk.at[s] if i == 0 else dst
        return pltpu.make_async_remote_copy(
            src_ref=src, dst_ref=dst, send_sem=send.at[s, i], recv_sem=recv.at[s, i],
            device_id=torus.neighbour(pos, core, ORDERS[s // 2][phase], d), device_id_type=MESH)

    def landed(s, i):
        phase, k = steps[s][i]
        d = 1 if s % 2 == 0 else -1
        here = region(s, phase, -d * (k + 1))
        return pltpu.make_async_remote_copy(
            src_ref=here, dst_ref=here, send_sem=send.at[s, i], recv_sem=recv.at[s, i],
            device_id=sibling, device_id_type=MESH), here

    def across(s, src, dst):
        return pltpu.make_async_remote_copy(
            src_ref=src, dst_ref=dst, send_sem=sib_send.at[s], recv_sem=sib_recv.at[s],
            device_id=sibling, device_id_type=MESH)

    for s in range(NS):
        ring(s, 0).start()
    for s in range(NS):
        pltpu.make_async_copy(blk.at[s], own[s], loc.at[s]).start()
        across(s, blk.at[s], own[s]).start()
    for s in range(NS):
        pltpu.make_async_copy(blk.at[s], own[s], loc.at[s]).wait()
    for s, i in torus.events(ORDERS, False):
        arrived, here = landed(s, i)
        arrived.wait_recv()
        if i + 1 < len(steps[s]):
            ring(s, i + 1).start()
        across(s, here, here).start()
    for s in range(NS):
        for i in range(len(steps[s])):
            ring(s, i).wait_send()
        whole = cut(torus, out, width, core, s, {})
        other = cut(torus, out, width, 1 - core, s, {})
        across(s, whole, whole).wait_send()
        across(s, other, other).wait_recv()


def gather_all(torus, blk):
    width = blk.shape[2]
    n = torus.n
    shape = (torus.nzl, torus.nzh, n["y"], 2, NS, OCT, n["x"] * width)
    count = len(torus.steps(ORDERS[0]))
    dma = pltpu.SemaphoreType.DMA
    return pl.pallas_call(
        functools.partial(gather_kernel, torus, width),
        out_shape=jax.ShapeDtypeStruct(shape, blk.dtype),
        in_specs=[pl.BlockSpec(memory_space=pltpu.VMEM)],
        out_specs=pl.BlockSpec(memory_space=pl.ANY),
        scratch_shapes=[dma((NS,)), dma((NS, count)), dma((NS, count)), dma((NS,)), dma((NS,))],
        compiler_params=pltpu.CompilerParams(collective_id=0, has_side_effects=True),
        name="gather_all",
    )(blk)


def back_orders():
    return tuple(tuple(reversed(o)) for o in ORDERS)


def scatter_kernel(torus, width, part, out, mine, theirs, bufs, loc, send, recv, sib_send, sib_recv):
    pos, core = torus.here()
    sibling = torus.device(pos, 1 - core)
    greet(torus, pos, core)
    orders = back_orders()
    steps = [torus.steps(orders[s // 2]) for s in range(NS)]

    def place(s, phase, shift):
        order = orders[s // 2]
        at = dict(pos)
        for axis in order[phase + 1:]:
            at[axis] = None
        at[order[phase]] = torus.shift(pos, order[phase], shift)
        return at

    def slot(s, i):
        phase, k = steps[s][i]
        return bufs[s // 2 * 3 + phase].at[s % 2, k]

    def ring(s, i):
        phase, k = steps[s][i]
        d = 1 if s % 2 == 0 else -1
        src = cut(torus, mine, width, None, s, place(s, phase, -d * (k + 1)))
        return pltpu.make_async_remote_copy(
            src_ref=src, dst_ref=slot(s, i), send_sem=send.at[s, i], recv_sem=recv.at[s, i],
            device_id=torus.neighbour(pos, core, orders[s // 2][phase], d), device_id_type=MESH)

    def add(s, at, buf):
        zs = list(range(torus.n["z"])) if at["z"] is None else None
        ny = torus.n["y"]
        wide = torus.n["x"] * width
        nz = torus.n["z"] if zs else 1
        ys = ny if at["y"] is None else 1
        if at["x"] is None:
            col, cols = pl.ds(0, wide), wide
        else:
            col, cols = pl.ds(pl.multiple_of(at["x"] * width, LANE), width), width

        def one(i, carry):
            iz, iy = lax.div(i, ys), lax.rem(i, ys)
            if at["z"] is None:
                zl, zh = lax.div(iz, torus.nzh), lax.rem(iz, torus.nzh)
                where = (zl, zh)
            else:
                zl, zh = lax.rem(at["z"], torus.nzl), lax.div(at["z"], torus.nzl)
                where = ()
            if at["y"] is None:
                y = iy
                where = where + (iy,)
            else:
                y = at["y"]
            got = buf[where + (slice(None), slice(None))].astype(F32)
            had = mine[zl, zh, y, s, :, col].astype(F32)
            mine[zl, zh, y, s, :, col] = (had + got).astype(BF16)
            return carry

        lax.fori_loop(0, nz * ys, one, 0)

    def fetch(s):
        return pltpu.make_async_copy(
            cut(torus, part, width, core, s, {}), cut(torus, mine, width, None, s, {}), loc.at[s])

    def across(s):
        return pltpu.make_async_remote_copy(
            src_ref=cut(torus, part, width, 1 - core, s, {}), dst_ref=cut(torus, theirs, width, None, s, {}),
            send_sem=sib_send.at[s], recv_sem=sib_recv.at[s], device_id=sibling, device_id_type=MESH)

    for s in range(NS):
        across(s).start()
        fetch(s).start()
    for s in range(NS):
        fetch(s).wait()
        across(s).wait_recv()
        add(s, {"x": None, "y": None, "z": None}, theirs.at[:, :, :, s])
        ring(s, 0).start()
    for s, i in torus.events(orders, True):
        ring(s, i).wait_recv()
        phase, k = steps[s][i]
        d = 1 if s % 2 == 0 else -1
        add(s, place(s, phase, -d * (k + 2)), slot(s, i))
        if i + 1 < len(steps[s]):
            ring(s, i + 1).start()
    zl, zh = lax.rem(pos["z"], torus.nzl), lax.div(pos["z"], torus.nzl)
    for s in range(NS):
        out[s] = mine[zl, zh, pos["y"], s, :, pl.ds(pl.multiple_of(pos["x"] * width, LANE), width)]
    for s in range(NS):
        across(s).wait_send()
        for i in range(len(steps[s])):
            ring(s, i).wait_send()


def scatter_kernel_flat(torus, width, part, out, mine, theirs, b0, b1, b2, b3, b4, b5, b6, b7, b8, *sems):
    scatter_kernel(torus, width, part, out, mine, theirs, (b0, b1, b2, b3, b4, b5, b6, b7, b8), *sems)


def scatter_all(torus, part):
    n = torus.n
    width = part.shape[6] // n["x"]
    half = (torus.nzl, torus.nzh, n["y"], NS, OCT, n["x"] * width)
    orders = back_orders()
    bufs = []
    for order in orders:
        for phase, axis in enumerate(order):
            free = order[phase + 1:]
            shape = (2, n[axis] - 1)
            if "z" in free:
                shape += (torus.nzl, torus.nzh)
            if "y" in free:
                shape += (n["y"],)
            shape += (OCT, n["x"] * width if "x" in free else width)
            bufs.append(pltpu.VMEM(shape, BF16))
    count = len(torus.steps(orders[0]))
    dma = pltpu.SemaphoreType.DMA
    return pl.pallas_call(
        functools.partial(scatter_kernel_flat, torus, width),
        out_shape=jax.ShapeDtypeStruct((NS, OCT, width), BF16),
        in_specs=[pl.BlockSpec(memory_space=pl.ANY)],
        out_specs=pl.BlockSpec(memory_space=pltpu.VMEM),
        scratch_shapes=[pltpu.VMEM(half, BF16), pltpu.VMEM(half, BF16), *bufs,
                        dma((NS,)), dma((NS, count)), dma((NS, count)), dma((NS,)), dma((NS,))],
        compiler_params=pltpu.CompilerParams(
            collective_id=1, has_side_effects=True, vmem_limit_bytes=60 * 1024 * 1024),
        name="scatter_all",
    )(part)


NT = (((1,), (1,)), ((), ()))


def rows_kernel(depth, n_et, x_ref, dy_ref, pick_ref, wg_ref, wu_ref, wd_ref, gt_ref, wt_ref, part_ref, wcat):
    @pl.when(pl.program_id(0) == 0)
    def _():
        wcat[:, :LANE] = wg_ref[...]
        wcat[:, LANE:] = wu_ref[...]

    pre = jnp.dot(x_ref[0, :, :depth], wcat[...], preferred_element_type=F32)
    back = lax.dot_general(dy_ref[0, :, :depth], wd_ref[...], NT, preferred_element_type=F32)
    gate_pre, up_pre = pre[:, :LANE], pre[:, LANE:]
    pick = pick_ref[...]
    scale = jnp.sum(x_ref[0, :, depth:depth + LANE].astype(F32) * pick, axis=1, keepdims=True)
    sigma = jax.nn.sigmoid(gate_pre)
    silu = gate_pre * sigma
    act = silu * up_pre
    score = jnp.sum(act * back, axis=1, keepdims=True)
    dact = scale * back
    grad_gate = dact * up_pre * sigma * (1.0 + gate_pre * (1.0 - sigma))
    grad_up = dact * silu
    both = jnp.concatenate([grad_gate, grad_up], axis=1)
    gt_ref[...] = both.T.astype(BF16)
    wt_ref[...] = (scale * act).T.astype(BF16)
    both = both.astype(BF16)
    cols = depth // n_et
    width = cols + LANE
    for j in range(n_et):
        piece = lax.dot_general(both, wcat[j * cols:(j + 1) * cols, :], NT, preferred_element_type=F32)
        part_ref[j // (n_et // 2), :, (j % (n_et // 2)) * width:(j % (n_et // 2)) * width + cols] = piece.astype(BF16)
        tail = score * pick if j == 0 else jnp.zeros((piece.shape[0], LANE), F32)
        part_ref[j // (n_et // 2), :, (j % (n_et // 2)) * width + cols:(j % (n_et // 2) + 1) * width] = tail.astype(BF16)


def rows_stage(everyone, pick, wg, wu, wd, n_et, tile):
    depth = wg.shape[0]
    rows, wide = everyone.shape[1:]
    out_wide = (depth // n_et + LANE) * (n_et // 2)
    whole = functools.partial(pl.BlockSpec, pipeline_mode=pl.Buffered(1))
    return pl.pallas_call(
        functools.partial(rows_kernel, depth, n_et),
        grid=(rows // tile,),
        in_specs=[
            pl.BlockSpec((1, tile, wide), lambda i: (0, i, 0)),
            pl.BlockSpec((1, tile, wide), lambda i: (1, i, 0)),
            whole((1, LANE), lambda i: (0, 0)),
            whole((depth, LANE), lambda i: (0, 0)),
            whole((depth, LANE), lambda i: (0, 0)),
            whole((LANE, depth), lambda i: (0, 0)),
        ],
        out_specs=[
            pl.BlockSpec((2 * LANE, tile), lambda i: (0, i)),
            pl.BlockSpec((LANE, tile), lambda i: (0, i)),
            pl.BlockSpec((2, tile, out_wide), lambda i: (0, i, 0)),
        ],
        out_shape=[
            jax.ShapeDtypeStruct((2 * LANE, rows), BF16),
            jax.ShapeDtypeStruct((LANE, rows), BF16),
            jax.ShapeDtypeStruct((2, rows, out_wide), BF16),
        ],
        scratch_shapes=[pltpu.VMEM((depth, 2 * LANE), BF16)],
        compiler_params=pltpu.CompilerParams(vmem_limit_bytes=60 * 1024 * 1024),
        name="rows_stage",
    )(everyone, everyone, pick, wg, wu, wd)


def weights_kernel(x_ref, dy_ref, gt_ref, wt_ref, dg_ref, du_ref, dd_ref):
    both = jnp.dot(gt_ref[...], x_ref[0], preferred_element_type=F32).T
    dg_ref[...] = both[:, :LANE].astype(BF16)
    du_ref[...] = both[:, LANE:].astype(BF16)
    dd_ref[...] = jnp.dot(wt_ref[...], dy_ref[0], preferred_element_type=F32).astype(BF16)


def weights_stage(everyone, gt, wt, depth, tile):
    rows = everyone.shape[1]
    return pl.pallas_call(
        weights_kernel,
        grid=(depth // tile,),
        in_specs=[
            pl.BlockSpec((1, rows, tile), lambda i: (0, 0, i)),
            pl.BlockSpec((1, rows, tile), lambda i: (1, 0, i)),
            pl.BlockSpec((2 * LANE, rows), lambda i: (0, 0), pipeline_mode=pl.Buffered(1)),
            pl.BlockSpec((LANE, rows), lambda i: (0, 0), pipeline_mode=pl.Buffered(1)),
        ],
        out_specs=[
            pl.BlockSpec((tile, LANE), lambda i: (i, 0)),
            pl.BlockSpec((tile, LANE), lambda i: (i, 0)),
            pl.BlockSpec((LANE, tile), lambda i: (0, i)),
        ],
        out_shape=[
            jax.ShapeDtypeStruct((depth, LANE), BF16),
            jax.ShapeDtypeStruct((depth, LANE), BF16),
            jax.ShapeDtypeStruct((LANE, depth), BF16),
        ],
        compiler_params=pltpu.CompilerParams(vmem_limit_bytes=60 * 1024 * 1024),
        name="weights_stage",
    )(everyone, everyone, gt, wt)


def on_device(torus, tokens, grad_out, gates, expert_ids, gate_weight, up_weight, down_weight):
    count, depth = tokens.shape
    n_exp = lax.axis_size("exp")
    n_et = lax.axis_size("et")
    experts = jnp.arange(LANE, dtype=jnp.int32)
    chosen = expert_ids[:, :, None] == experts[None, None, :]
    table = jnp.sum(jnp.where(chosen, gates[:, :, None].astype(F32), 0.0), axis=1).astype(BF16)
    half = -(-(depth + LANE) // (n_et // 2 * LANE)) * (n_et // 2 * LANE)
    packed = jnp.concatenate([
        tokens, table, jnp.zeros((count, half - depth - LANE), BF16),
        grad_out, jnp.zeros((count, half - depth), BF16)], axis=1)
    blk = lax.all_to_all(packed, "et", split_axis=1, concat_axis=0, tiled=True)
    blk = blk.reshape(NS, OCT, blk.shape[1])
    everyone = gather_all(torus, blk)
    rows = n_exp * n_et * count
    everyone = everyone.reshape(2, rows, half)
    pick = (experts == lax.axis_index("exp")).astype(F32)[None, :]
    wg, wu, wd = gate_weight[0], up_weight[0], down_weight[0]
    gt, wt, part = rows_stage(everyone, pick, wg, wu, wd, n_et, 256 if rows % 256 == 0 else 128)
    part = part.reshape(torus.nzl, torus.nzh, torus.n["y"], 2, NS, OCT, part.shape[2])
    mine = scatter_all(torus, part)
    mine = mine.reshape(NS * OCT, mine.shape[2])
    owned = lax.all_to_all(mine, "et", split_axis=0, concat_axis=1, tiled=True)
    owned = owned.reshape(count, n_et, owned.shape[1] // n_et)
    cols = depth // n_et
    input_grad = owned[:, :, :cols].reshape(count, depth)
    scores = owned[:, 0, cols:].astype(F32)
    gate_grad = jnp.sum(jnp.where(chosen, scores[:, None, :], 0.0), axis=2)
    dg, du, dd = weights_stage(everyone, gt, wt, depth, min(512, depth))
    return input_grad, gate_grad, dg[None], du[None], dd[None]


def solution(mesh, dims=(4, 4, 4, 2)):
    placed = (
        P(("exp", "et"), None),
        P(("exp", "et"), None),
        P(("exp", "et"), None),
        P(("exp", "et"), None),
        P("exp", None, "et"),
        P("exp", None, "et"),
        P("exp", "et", None),
    )
    return jax.shard_map(
        functools.partial(on_device, Torus(*dims)),
        mesh=mesh,
        in_specs=placed,
        out_specs=(
            P(("exp", "et"), None),
            P(("exp", "et"), None),
            P("exp", None, "et"),
            P("exp", None, "et"),
            P("exp", "et", None),
        ),
        check_vma=False,
    )
```

```python
import functools
import jax
import jax.numpy as jnp
from jax import lax
from jax.experimental import pallas as pl
from jax.experimental.pallas import tpu as pltpu
from jax.sharding import PartitionSpec as P

TOP = 8
LANE = 128
NS = 6
OCT = 8
MESH = pl.DeviceIdType.MESH
ORDERS = (("x", "y", "z"), ("z", "y", "x"), ("z", "x", "y"))
ROWS = 16
NT = (((1,), (1,)), ((), ()))
F32 = jnp.float32
BF16 = jnp.bfloat16


class Torus:
    def __init__(self, nx, ny, nzh, nzl):
        self.n = {"x": nx, "y": ny, "z": nzh * nzl}
        self.nzh, self.nzl = nzh, nzl

    def here(self):
        e = lax.axis_index("exp")
        t = lax.axis_index("et")
        ny, nx = self.n["y"], self.n["x"]
        core = lax.rem(e, 2)
        y = lax.rem(lax.div(e, 2), ny)
        zh = lax.div(e, 2 * ny)
        x = lax.rem(t, nx)
        zl = lax.div(t, nx)
        return {"x": x, "y": y, "z": zh * self.nzl + zl}, core

    def split(self, z):
        return lax.rem(z, self.nzl), lax.div(z, self.nzl)

    def device(self, pos, core):
        zl, zh = self.split(pos["z"])
        return {
            "exp": (zh * self.n["y"] + pos["y"]) * 2 + core,
            "et": zl * self.n["x"] + pos["x"],
        }

    def shift(self, pos, axis, by):
        n = self.n[axis]
        return lax.rem(pos[axis] + (by % n + n), n)

    def moved(self, pos, axis, by):
        other = dict(pos)
        other[axis] = self.shift(pos, axis, by)
        return other

    def experts(self):
        return [(c, y, h) for c in range(2) for y in range(self.n["y"]) for h in range(self.nzh) if c or y or h]

    def other_expert(self, pos, core, offset, sign):
        c, y, h = offset
        out = self.moved(pos, "y", sign * y)
        out["z"] = self.shift(pos, "z", sign * h * self.nzl)
        return out, (1 - core if c else core)

    def greet(self, pos, core):
        seen, partners = set(), []
        for c, y, h in self.experts():
            p, k = self.other_expert(pos, core, (c, y, h), 1)
            partners.append(self.device(p, k))
            if not c and not y:
                seen.add(("z", h * self.nzl))
            if not c and not h:
                seen.add(("y", y))
        for axis in "xyz":
            for by in range(1, self.n[axis]):
                if (axis, by) not in seen:
                    partners.append(self.device(self.moved(pos, axis, by), core))
        barrier = pltpu.get_barrier_semaphore()
        for p in partners:
            pl.semaphore_signal(barrier, inc=1, device_id=p, device_id_type=MESH)
        pl.semaphore_wait(barrier, len(partners))


def remote(src, dst, send, recv, device):
    return pltpu.make_async_remote_copy(
        src_ref=src, dst_ref=dst, send_sem=send, recv_sem=recv, device_id=device, device_id_type=MESH)


def chosen_part(torus, at, part, width):
    zl, zh, y = slice(None), slice(None), slice(None)
    if at["z"] is not None:
        zl, zh = torus.split(at["z"])
    if at["y"] is not None:
        y = at["y"]
    col = slice(None)
    if at["x"] is not None:
        col = pl.ds(pl.multiple_of(at["x"] * width, LANE), width)
    if part is not None:
        if at["z"] is None:
            zl = part
        elif at["y"] is None:
            n = torus.n["y"] // 2
            y = pl.ds(part * n, n)
        else:
            n = torus.n["x"] // 2 * width
            col = pl.ds(part * n, n)
    return zl, zh, y, col


def volume(torus, axes):
    w = 1
    for a in axes:
        w *= torus.n[a]
    return w


def gather_kernel(torus, width, blk, sel, out, gate_out, gate_in, loc, p1_send, p1_recv, send, recv, sib_send,
                  sib_recv, g_send, g_recv):
    pos, core = torus.here()
    me = torus.device(pos, core)["exp"]
    sibling = torus.device(pos, 1 - core)
    torus.greet(pos, core)

    def region(s, phase, shift, part=None, c=core):
        order = ORDERS[s // 2]
        at = dict(pos)
        for axis in order[:phase]:
            at[axis] = None
        if phase < 3:
            at[order[phase]] = torus.shift(pos, order[phase], shift)
        zl, zh, y, col = chosen_part(torus, at, part, width)
        return out.at[zl, s % 2, zh, y, c, s // 2, :, col]

    def first(s, by):
        axis = ORDERS[s // 2][0]
        return remote(blk.at[s % 2, s // 2], region(s, 0, 0), p1_send.at[s, by - 1], p1_recv.at[s, by - 1],
                      torus.device(torus.moved(pos, axis, by), core))

    def first_landed(s, by):
        here = region(s, 0, -by)
        return remote(here, here, p1_send.at[s, by - 1], p1_recv.at[s, by - 1], sibling)

    def ring(s, phase, k, part):
        d = 1 if s % 2 == 0 else -1
        here = region(s, phase, -d * k, part)
        i = phase - 1
        return remote(here, here, send.at[s, i, k, part], recv.at[s, i, k, part],
                      torus.device(torus.moved(pos, ORDERS[s // 2][phase], d), core))

    def landed(s, phase, k, part):
        d = 1 if s % 2 == 0 else -1
        here = region(s, phase, -d * (k + 1), part)
        return remote(here, here, send.at[s, phase - 1, k, part], recv.at[s, phase - 1, k, part], sibling)

    def across(s, src, dst):
        return remote(src, dst, sib_send.at[s], sib_recv.at[s], sibling)

    def own(s):
        return pltpu.make_async_copy(blk.at[s % 2, s // 2], region(s, 0, 0), loc.at[s])

    for s in range(NS):
        for by in range(1, torus.n[ORDERS[s // 2][0]]):
            first(s, by).start()
        own(s).start()
    for q, offset in enumerate(torus.experts()):
        p, k = torus.other_expert(pos, core, offset, 1)
        to = torus.device(p, k)
        remote(sel.at[to["exp"]], gate_in.at[me], g_send.at[q], g_recv.at[q], to).start()
    gate_in[me] = sel[me]
    for s in range(NS):
        own(s).wait()
        for by in range(1, torus.n[ORDERS[s // 2][0]]):
            first_landed(s, by).wait_recv()
        for part in range(2):
            ring(s, 1, 0, part).start()
        whole = region(s, 1, 0)
        across(s, whole, whole).start()
    events = []
    for s in range(NS):
        order = ORDERS[s // 2]
        at = 0.0
        for phase in (1, 2):
            w = volume(torus, order[:phase]) * (1.5 if phase == 1 else 1.0)
            for k in range(torus.n[order[phase]] - 1):
                for part in range(2):
                    at += w / 2 + 0.5
                    events.append((at, s, phase, k, part))
            at += 1.0
    for _, s, phase, k, part in sorted(events):
        order = ORDERS[s // 2]
        arrived = landed(s, phase, k, part)
        arrived.wait_recv()
        if k + 1 < torus.n[order[phase]] - 1:
            ring(s, phase, k + 1, part).start()
        elif phase == 1 and part == 1:
            for half in range(2):
                ring(s, 2, 0, half).start()
        d = 1 if s % 2 == 0 else -1
        here = region(s, phase, -d * (k + 1), part)
        across(s, here, here).start()
    for q, offset in enumerate(torus.experts()):
        p, k = torus.other_expert(pos, core, offset, -1)
        came = torus.device(p, k)
        remote(sel.at[me], gate_in.at[came["exp"]], g_send.at[q], g_recv.at[q], came).wait_recv()
    gate_out[...] = gate_in[...]
    for s in range(NS):
        order = ORDERS[s // 2]
        for by in range(1, torus.n[order[0]]):
            first(s, by).wait_send()
        for phase in (1, 2):
            for k in range(torus.n[order[phase]] - 1):
                for part in range(2):
                    ring(s, phase, k, part).wait_send()
        whole, other = region(s, 3, 0), region(s, 3, 0, None, 1 - core)
        across(s, whole, whole).wait_send()
        across(s, other, other).wait_recv()
    for q, offset in enumerate(torus.experts()):
        p, k = torus.other_expert(pos, core, offset, 1)
        to = torus.device(p, k)
        remote(sel.at[to["exp"]], gate_in.at[me], g_send.at[q], g_recv.at[q], to).wait_send()


def gather_all(torus, blk, sel):
    width = blk.shape[3]
    n = torus.n
    shape = (torus.nzl, 2, torus.nzh, n["y"], 2, NS // 2, ROWS, n["x"] * width)
    most = max(n.values()) - 1
    others = len(torus.experts())
    dma = pltpu.SemaphoreType.DMA
    return pl.pallas_call(
        functools.partial(gather_kernel, torus, width),
        out_shape=[jax.ShapeDtypeStruct(shape, blk.dtype), jax.ShapeDtypeStruct(sel.shape, sel.dtype)],
        in_specs=[pl.BlockSpec(memory_space=pltpu.VMEM)] * 2,
        out_specs=[pl.BlockSpec(memory_space=pl.ANY), pl.BlockSpec(memory_space=pltpu.VMEM)],
        scratch_shapes=[pltpu.VMEM(sel.shape, sel.dtype), dma((NS,)), dma((NS, most)), dma((NS, most)),
                        dma((NS, 2, most, 2)), dma((NS, 2, most, 2)), dma((NS,)), dma((NS,)),
                        dma((others,)), dma((others,))],
        compiler_params=pltpu.CompilerParams(collective_id=0, has_side_effects=True),
        name="gather_all",
    )(blk, sel)


BACK = tuple(tuple(reversed(o)) for o in ORDERS)


def back_kernel(torus, depth, tile_cols, every, gates, wg, wu, wd, out, score_out, dg, du, dd,
                part, theirs, wcat, wdown, gt, wt, score, score_in, b0, b1, b2, b3, b4, b5, b6, b7, b8,
                w_sem, sib_send, sib_recv, send, recv, p3_send, p3_recv, s_send, s_recv):
    bufs = (b0, b1, b2, b3, b4, b5, b6, b7, b8)
    n = torus.n
    width = depth // (torus.nzl * n["x"])
    wide = n["x"] * width
    pos, core = torus.here()
    me = torus.device(pos, core)["exp"]
    sibling = torus.device(pos, 1 - core)
    hz = torus.nzh // 2
    group = hz * n["y"] * 2
    rows = group * ROWS
    tiles = NS
    half = depth // 2

    loads = [pltpu.make_async_copy(wg, wcat.at[:, pl.ds(0, LANE)], w_sem.at[0]),
             pltpu.make_async_copy(wu, wcat.at[:, pl.ds(LANE, LANE)], w_sem.at[1]),
             pltpu.make_async_copy(wd, wdown, w_sem.at[2])]
    for c in loads:
        c.start()

    def block(at, s, k=core):
        zl, zh, y, col = chosen_part(torus, at, None, width)
        return part.at[k, zl, zh, y, s, :, col]

    def place(s, phase, shift):
        order = BACK[s // 2]
        at = dict(pos)
        for axis in order[phase + 1:]:
            at[axis] = None
        at[order[phase]] = torus.shift(pos, order[phase], shift)
        return at

    def piece(at, s, h):
        zl, zh, y, col = chosen_part(torus, at, h, width)
        return part.at[core, zl, zh, y, s, :, col]

    def slot(s, phase, k, h):
        ref = bufs[s // 2 * 3 + phase].at[s % 2, k]
        if h is None:
            return ref
        order = BACK[s // 2]
        if "z" in order[phase + 1:]:
            return ref.at[h]
        if "y" in order[phase + 1:]:
            return ref.at[pl.ds(h * (n["y"] // 2), n["y"] // 2)]
        return ref.at[:, pl.ds(h * (n["x"] // 2) * width, n["x"] // 2 * width)]

    def ring(s, phase, k, h):
        d = 1 if s % 2 == 0 else -1
        return remote(piece(place(s, phase, -d * (k + 1)), s, h), slot(s, phase, k, h),
                      send.at[s, phase, k, h], recv.at[s, phase, k, h],
                      torus.device(torus.moved(pos, BACK[s // 2][phase], d), core))

    def last(s, by):
        axis = BACK[s // 2][2]
        return remote(block(place(s, 2, by), s), bufs[s // 2 * 3 + 2].at[s % 2, by - 1],
                      p3_send.at[s, by - 1], p3_recv.at[s, by - 1],
                      torus.device(torus.moved(pos, axis, by), core))

    def add(s, at, got, h):
        zl0, zh0, y0, col0 = None, None, None, None
        nzl, nzh, ny = 1, 1, 1
        zbase = ybase = 0
        if at["z"] is None:
            nzh = torus.nzh
            nzl = torus.nzl if h is None else 1
            zbase = 0 if h is None else h
        else:
            zl0, zh0 = torus.split(at["z"])
        if at["y"] is None:
            ny = n["y"]
            if h is not None and at["z"] is not None:
                ny, ybase = n["y"] // 2, h * (n["y"] // 2)
        else:
            y0 = at["y"]
        if at["x"] is None:
            cols = wide
            col0 = pl.ds(0, wide)
            if h is not None and at["z"] is not None and at["y"] is not None:
                cols = wide // 2
                col0 = pl.ds(h * cols, cols)
        else:
            cols = width
            col0 = pl.ds(pl.multiple_of(at["x"] * width, LANE), width)

        def one(i, carry):
            iy = lax.rem(i, ny)
            iz = lax.div(i, ny)
            izh = lax.rem(iz, nzh)
            izl = lax.div(iz, nzh)
            where = ()
            if at["z"] is None:
                where = (izh,) if h is not None else (izl, izh)
                zl, zh = izl + zbase, izh
            else:
                zl, zh = zl0, zh0
            if at["y"] is None:
                where = where + (iy,)
                y = iy + ybase
            else:
                y = y0
            g = got[where + (slice(None), slice(None))].astype(F32)
            p = part[core, zl, zh, y, s, :, col0].astype(F32)
            part[core, zl, zh, y, s, :, col0] = (p + g).astype(BF16)
            return carry

        lax.fori_loop(0, nzl * nzh * ny, one, 0)

    def cross(t):
        o, hh = t // 2, t % 2
        zs, os = pl.ds(hh * hz, hz), pl.ds(2 * o, 2)
        return remote(part.at[1 - core, :, zs, :, os], theirs.at[:, zs, :, os], sib_send.at[t], sib_recv.at[t], sibling)

    everywhere = {"x": None, "y": None, "z": None}

    def begin(o):
        for t in (2 * o, 2 * o + 1):
            cross(t).wait_recv()
        for s in (2 * o, 2 * o + 1):
            add(s, everywhere, theirs.at[:, :, :, s], None)
            for h in range(2):
                ring(s, 0, 0, h).start()

    def rows_phase(xs, ds, x_sem, d_sem):
        def fetch(which, t):
            o, hh = t // 2, t % 2
            buf, sem = (xs, x_sem) if which == 0 else (ds, d_sem)
            return [pltpu.make_async_copy(every.at[which, d, pl.ds(hh * hz, hz), :, :, o], buf.at[d], sem.at[d])
                    for d in range(2)]

        for which in range(2):
            for c in fetch(which, 0):
                c.start()
        score[...] = jnp.zeros_like(score)
        torus.greet(pos, core)
        for c in loads:
            c.wait()
        for t in range(tiles):
            o, hh = t // 2, t % 2
            for c in fetch(0, t):
                c.wait()
            pre = jnp.dot(xs[0].reshape(rows, half), wcat[:half, :], preferred_element_type=F32)
            pre = pre + jnp.dot(xs[1].reshape(rows, half), wcat[half:, :], preferred_element_type=F32)
            if t + 1 < tiles:
                for c in fetch(0, t + 1):
                    c.start()
            for c in fetch(1, t):
                c.wait()
            back = lax.dot_general(ds[0].reshape(rows, half), wdown[:, :half], NT, preferred_element_type=F32)
            back = back + lax.dot_general(ds[1].reshape(rows, half), wdown[:, half:], NT, preferred_element_type=F32)
            if t + 1 < tiles:
                for c in fetch(1, t + 1):
                    c.start()
            gate_pre, up_pre = pre[:, :LANE], pre[:, LANE:]
            scale = gates[t]
            sigma = jax.nn.sigmoid(gate_pre)
            silu = gate_pre * sigma
            act = silu * up_pre
            dact = scale * back
            grad_gate = dact * up_pre * sigma * (1.0 + gate_pre * (1.0 - sigma))
            grad_up = dact * silu
            cols = pl.ds(t * rows, rows)
            gt[:LANE, cols] = grad_gate.T.astype(BF16)
            gt[LANE:, cols] = grad_up.T.astype(BF16)
            wt[:, cols] = (scale * act).T.astype(BF16)
            sums = jnp.sum((act * back).T, axis=0, keepdims=True)
            each = rows // hz
            for z in range(hz):
                score[hh * hz + z, o:o + 1, :each] = sums[:, z * each:(z + 1) * each]
            both = jnp.concatenate([grad_gate.astype(BF16), grad_up.astype(BF16)], axis=1)
            for j in range(torus.nzl * n["x"]):
                zl, x = j // n["x"], j % n["x"]
                grad = lax.dot_general(both, wcat[j * width:(j + 1) * width, :], NT, preferred_element_type=F32)
                grad = grad.reshape(hz, n["y"], 2, 2, OCT, width).astype(BF16)
                for k in range(2):
                    part[k, zl, hh * hz:(hh + 1) * hz, :, 2 * o:2 * o + 2, :, x * width:(x + 1) * width] = grad[:, :, k]
            cross(t).start()
            if t in (2, 4):
                begin(t // 2 - 1)

    pl.run_scoped(
        rows_phase,
        pltpu.VMEM((2, hz, n["y"], 2, ROWS, half), BF16), pltpu.VMEM((2, hz, n["y"], 2, ROWS, half), BF16),
        pltpu.SemaphoreType.DMA((2,)), pltpu.SemaphoreType.DMA((2,)))

    def message(q, offset, sign):
        p, k = torus.other_expert(pos, core, offset, sign)
        other = torus.device(p, k)
        zh = torus.split(p["z"])[1]
        mine = score.at[zh] if sign > 0 else score.at[0]
        return remote(mine, score_in.at[me if sign > 0 else other["exp"]], s_send.at[q], s_recv.at[q], other)

    for q, offset in enumerate(torus.experts()):
        message(q, offset, 1).start()
    score_in[me] = score[torus.split(pos["z"])[1]]

    def exchange(xt, dt, sg, su, sd, x_sem, d_sem, o_sem):
        units = depth // tile_cols
        per = half // tile_cols

        def fetch(u, which):
            buf, sem = (xt, x_sem) if which == 0 else (dt, d_sem)
            d, c = u // per, pl.ds(u % per * tile_cols, tile_cols)
            return [pltpu.make_async_copy(every.at[which, d, pl.ds(t % 2 * hz, hz), :, :, t // 2, :, c],
                                          buf.at[u % 2, t], sem.at[u % 2, t]) for t in range(tiles)]

        def put(u):
            c = pl.ds(u * tile_cols, tile_cols)
            return [pltpu.make_async_copy(sg.at[u % 2], dg.at[c], o_sem.at[u % 2, 0]),
                    pltpu.make_async_copy(su.at[u % 2], du.at[c], o_sem.at[u % 2, 1]),
                    pltpu.make_async_copy(sd.at[u % 2], dd.at[:, c], o_sem.at[u % 2, 2])]

        def get(u):
            for which in range(2):
                for c in fetch(u, which):
                    c.start()

        def unit(u):
            if u + 1 < units:
                get(u + 1)
            for which in range(2):
                for c in fetch(u, which):
                    c.wait()
            if u >= 2:
                for c in put(u - 2):
                    c.wait()
            both = jnp.dot(gt[...], xt[u % 2].reshape(tiles * rows, tile_cols), preferred_element_type=F32).T
            sg[u % 2] = both[:, :LANE].astype(BF16)
            su[u % 2] = both[:, LANE:].astype(BF16)
            down = jnp.dot(wt[...], dt[u % 2].reshape(tiles * rows, tile_cols), preferred_element_type=F32)
            sd[u % 2] = down.astype(BF16)
            for c in put(u):
                c.start()

        get(0)
        begin(2)
        events = []
        for s in range(NS):
            order = BACK[s // 2]
            at = (s // 2) * 3.0
            for phase in (0, 1):
                w = volume(torus, order[phase + 1:])
                for k in range(n[order[phase]] - 1):
                    for h in range(2):
                        at += w / 2 + 0.5
                        events.append((at, s, phase, k, h))
                at += 2.0
            events.append((at + 6.0, s, 2, 0, 0))
        events.sort()
        done = 0
        for i, (_, s, phase, k, h) in enumerate(events):
            while done < units and done * len(events) * 3 // 5 <= i * units:
                unit(done)
                done += 1
            order = BACK[s // 2]
            d = 1 if s % 2 == 0 else -1
            if phase < 2:
                ring(s, phase, k, h).wait_recv()
                add(s, place(s, phase, -d * (k + 2)), slot(s, phase, k, h), h)
                if k + 1 < n[order[phase]] - 1:
                    ring(s, phase, k + 1, h).start()
                elif h == 1 and phase == 0:
                    for hh in range(2):
                        ring(s, 1, 0, hh).start()
                elif h == 1:
                    for by in range(1, n[order[2]]):
                        last(s, by).start()
            else:
                zl, zh = torus.split(pos["z"])
                col = pl.ds(pl.multiple_of(pos["x"] * width, LANE), width)
                total = part[core, zl, zh, pos["y"], s, :, col].astype(F32)
                for by in range(1, n[order[2]]):
                    last(s, by).wait_recv()
                    total = total + bufs[s // 2 * 3 + 2][s % 2, by - 1].astype(F32)
                out[s] = total.astype(BF16)
        while done < units:
            unit(done)
            done += 1
        for u in (units - 2, units - 1):
            for c in put(u):
                c.wait()

    stage = pltpu.VMEM((2, tile_cols, LANE), BF16)
    tiled = pltpu.VMEM((2, tiles, hz, n["y"], 2, ROWS, tile_cols), BF16)
    dma = pltpu.SemaphoreType.DMA
    pl.run_scoped(exchange, tiled, tiled, stage, stage, pltpu.VMEM((2, LANE, tile_cols), BF16),
                  dma((2, tiles)), dma((2, tiles)), dma((2, 3)))

    for q, offset in enumerate(torus.experts()):
        message(q, offset, -1).wait_recv()
    score_out[...] = score_in[...]
    for q, offset in enumerate(torus.experts()):
        message(q, offset, 1).wait_send()
    for t in range(tiles):
        cross(t).wait_send()
    for s in range(NS):
        order = BACK[s // 2]
        for phase in (0, 1):
            for k in range(n[order[phase]] - 1):
                for h in range(2):
                    ring(s, phase, k, h).wait_send()
        for by in range(1, n[order[2]]):
            last(s, by).wait_send()


def back_all(torus, every, gates, wg, wu, wd):
    n = torus.n
    depth = wg.shape[0]
    width = depth // (torus.nzl * n["x"])
    wide = n["x"] * width
    experts = torus.nzh * n["y"] * 2
    bufs = []
    for order in BACK:
        for phase, axis in enumerate(order):
            free = order[phase + 1:]
            shape = (2, n[axis] - 1)
            if "z" in free:
                shape += (torus.nzl, torus.nzh)
            if "y" in free:
                shape += (n["y"],)
            shape += (OCT, wide if "x" in free else width)
            bufs.append(pltpu.VMEM(shape, BF16))
    most = max(n.values()) - 1
    others = len(torus.experts())
    total = experts * NS * OCT
    dma = pltpu.SemaphoreType.DMA
    vm = pltpu.VMEM
    half = (torus.nzl, torus.nzh, n["y"], NS, OCT, wide)
    any_ = pl.BlockSpec(memory_space=pl.ANY)
    vspec = pl.BlockSpec(memory_space=pltpu.VMEM)
    return pl.pallas_call(
        functools.partial(back_kernel, torus, depth, min(512, depth // 2)),
        out_shape=[jax.ShapeDtypeStruct((NS, OCT, width), BF16),
                   jax.ShapeDtypeStruct((experts, OCT, LANE), F32),
                   jax.ShapeDtypeStruct((depth, LANE), BF16),
                   jax.ShapeDtypeStruct((depth, LANE), BF16),
                   jax.ShapeDtypeStruct((LANE, depth), BF16)],
        in_specs=[any_, vspec, any_, any_, any_],
        out_specs=[vspec, vspec, any_, any_, any_],
        scratch_shapes=[vm((2,) + half, BF16), vm(half, BF16), vm((depth, 2 * LANE), BF16), vm((LANE, depth), BF16),
                        vm((2 * LANE, total), BF16), vm((LANE, total), BF16), vm((torus.nzh, OCT, LANE), F32),
                        vm((experts, OCT, LANE), F32), *bufs, dma((3,)), dma((NS,)), dma((NS,)),
                        dma((NS, 2, most, 2)), dma((NS, 2, most, 2)), dma((NS, most)), dma((NS, most)),
                        dma((others,)), dma((others,))],
        compiler_params=pltpu.CompilerParams(
            collective_id=1, has_side_effects=True, vmem_limit_bytes=67043328),
        name="back_all",
    )(every, gates, wg, wu, wd)


def on_device(torus, tokens, grad_out, gates, expert_ids, gate_weight, up_weight, down_weight):
    count, depth = tokens.shape
    n = torus.n
    n_et = torus.nzl * n["x"]
    n_exp = torus.nzh * n["y"] * 2
    share = depth // (2 * n["x"])
    experts = jnp.arange(LANE, dtype=jnp.int32)
    chosen = expert_ids[:, :, None] == experts[None, None, :]
    table = jnp.sum(jnp.where(chosen, gates[:, :, None].astype(F32), 0.0), axis=1).astype(BF16)
    packed = jnp.stack([tokens, grad_out], axis=1).reshape(count, 2, 2, n["x"], share)
    packed = packed.transpose(0, 1, 3, 2, 4).reshape(count, n_et, 2 * share)
    packed = jnp.concatenate([packed, jnp.broadcast_to(table[:, None], (count, n_et, LANE))], axis=2)
    blk = lax.all_to_all(packed.reshape(count, n_et * (2 * share + LANE)), "et", split_axis=1, concat_axis=0, tiled=True)
    rows = n_et * count
    sel = blk[:, 2 * share:].astype(F32).T[:n_exp]
    sel = jnp.pad(sel, ((0, 0), (0, LANE - rows)))[:, None, :]
    blk = blk[:, :2 * share].reshape(NS // 2, ROWS, 2, share).transpose(2, 0, 1, 3)
    every, scale = gather_all(torus, blk, sel)
    scale = scale[:, 0, :rows].reshape(2, n_exp // 2, NS // 2, ROWS).transpose(2, 0, 1, 3)
    scale = jnp.broadcast_to(scale.reshape(NS, n_exp // 2 * ROWS, 1), (NS, n_exp // 2 * ROWS, LANE))
    mine, score, dg, du, dd = back_all(torus, every, scale, gate_weight[0], up_weight[0], down_weight[0])
    me = lax.axis_index("exp")
    per = 2 * n["y"]
    score = score[:, :NS // 2, :per * ROWS].reshape(n_exp, NS // 2, per, ROWS)
    score = lax.dynamic_index_in_dim(score, lax.rem(me, per), axis=2, keepdims=False)
    score = jnp.pad(score.reshape(n_exp, rows).T.astype(BF16), ((0, 0), (0, LANE - n_exp)))
    mine = jnp.concatenate([mine.reshape(rows, mine.shape[2]), score], axis=1)
    owned = lax.all_to_all(mine, "et", split_axis=0, concat_axis=1, tiled=True)
    cols = depth // n_et
    owned = owned.reshape(count, n_et, cols + LANE)
    input_grad = owned[:, :, :cols].reshape(count, depth)
    scores = jnp.sum(owned[:, :, cols:].astype(F32), axis=1)
    gate_grad = jnp.sum(jnp.where(chosen, scores[:, None, :], 0.0), axis=2)
    return input_grad, gate_grad, dg[None], du[None], dd[None]


def solution(mesh, dims=(4, 4, 4, 2)):
    placed = (
        P(("exp", "et"), None),
        P(("exp", "et"), None),
        P(("exp", "et"), None),
        P(("exp", "et"), None),
        P("exp", None, "et"),
        P("exp", None, "et"),
        P("exp", "et", None),
    )
    return jax.shard_map(
        functools.partial(on_device, Torus(*dims)),
        mesh=mesh,
        in_specs=placed,
        out_specs=(
            P(("exp", "et"), None),
            P(("exp", "et"), None),
            P("exp", None, "et"),
            P("exp", None, "et"),
            P("exp", "et", None),
        ),
        check_vma=False,
    )
```

```python
import functools
import jax
import jax.numpy as jnp
from jax import lax
from jax.experimental import pallas as pl
from jax.experimental.pallas import tpu as pltpu
from jax.sharding import PartitionSpec as P

TOP = 8
LANE = 128
NS = 6
OCT = 8
MESH = pl.DeviceIdType.MESH
ORDERS = (("x", "y", "z"), ("z", "y", "x"), ("z", "x", "y"))
ROWS = 16
NT = (((1,), (1,)), ((), ()))
F32 = jnp.float32
BF16 = jnp.bfloat16


class Torus:
    def __init__(self, nx, ny, nzh, nzl):
        self.n = {"x": nx, "y": ny, "z": nzh * nzl}
        self.nzh, self.nzl = nzh, nzl

    def here(self):
        e = lax.axis_index("exp")
        t = lax.axis_index("et")
        ny, nx = self.n["y"], self.n["x"]
        core = lax.rem(e, 2)
        y = lax.rem(lax.div(e, 2), ny)
        zh = lax.div(e, 2 * ny)
        x = lax.rem(t, nx)
        zl = lax.div(t, nx)
        return {"x": x, "y": y, "z": zh * self.nzl + zl}, core

    def split(self, z):
        return lax.rem(z, self.nzl), lax.div(z, self.nzl)

    def device(self, pos, core):
        zl, zh = self.split(pos["z"])
        return {
            "exp": (zh * self.n["y"] + pos["y"]) * 2 + core,
            "et": zl * self.n["x"] + pos["x"],
        }

    def shift(self, pos, axis, by):
        n = self.n[axis]
        return lax.rem(pos[axis] + (by % n + n), n)

    def moved(self, pos, axis, by):
        other = dict(pos)
        other[axis] = self.shift(pos, axis, by)
        return other

    def experts(self):
        return [(c, y, h) for c in range(2) for y in range(self.n["y"]) for h in range(self.nzh) if c or y or h]

    def other_expert(self, pos, core, offset, sign):
        c, y, h = offset
        out = self.moved(pos, "y", sign * y)
        out["z"] = self.shift(pos, "z", sign * h * self.nzl)
        return out, (1 - core if c else core)

    def peers(self):
        return [(l, x) for l in range(self.nzl) for x in range(self.n["x"]) if l or x]

    def peer(self, pos, core, offset, sign):
        l, x = offset
        out = self.moved(pos, "x", sign * x)
        zl, zh = self.split(pos["z"])
        out["z"] = zh * self.nzl + (lax.rem(zl + l, self.nzl) if l else zl)
        return self.device(out, core)

    def greet(self, pos, core):
        seen, partners = set(), []
        for c, y, h in self.experts():
            p, k = self.other_expert(pos, core, (c, y, h), 1)
            partners.append(self.device(p, k))
            if not c and not y:
                seen.add(("z", h * self.nzl))
            if not c and not h:
                seen.add(("y", y))
        for axis in "xyz":
            for by in range(1, self.n[axis]):
                if (axis, by) not in seen:
                    partners.append(self.device(self.moved(pos, axis, by), core))
        for l, x in self.peers():
            if l and x:
                partners.append(self.peer(pos, core, (l, x), 1))
        barrier = pltpu.get_barrier_semaphore()
        for p in partners:
            pl.semaphore_signal(barrier, inc=1, device_id=p, device_id_type=MESH)
        pl.semaphore_wait(barrier, len(partners))


def remote(src, dst, send, recv, device):
    return pltpu.make_async_remote_copy(
        src_ref=src, dst_ref=dst, send_sem=send, recv_sem=recv, device_id=device, device_id_type=MESH)


def chosen_part(torus, at, part, width):
    zl, zh, y = slice(None), slice(None), slice(None)
    if at["z"] is not None:
        zl, zh = torus.split(at["z"])
    if at["y"] is not None:
        y = at["y"]
    col = slice(None)
    if at["x"] is not None:
        col = pl.ds(pl.multiple_of(at["x"] * width, LANE), width)
    if part is not None:
        if at["z"] is None:
            zl = part
        elif at["y"] is None:
            n = torus.n["y"] // 2
            y = pl.ds(part * n, n)
        else:
            n = torus.n["x"] // 2 * width
            col = pl.ds(part * n, n)
    return zl, zh, y, col


def volume(torus, axes):
    w = 1
    for a in axes:
        w *= torus.n[a]
    return w


def gather_kernel(torus, width, packed, sel, out, gate_out, gate_in, gate_all, inbox, stack, blk, loc, p1_send, p1_recv,
                  send, recv, sib_send, sib_recv, g_send, g_recv, e_send, e_recv, h_send, h_recv):
    pos, core = torus.here()
    me = torus.device(pos, core)["exp"]
    my_et = torus.device(pos, core)["et"]
    sibling = torus.device(pos, 1 - core)
    torus.greet(pos, core)

    def hand(q, offset, sign):
        to = torus.peer(pos, core, offset, sign)
        slot = my_et if sign > 0 else to["et"]
        return remote(packed.at[to["et"]], inbox.at[slot], e_send.at[q], e_recv.at[q], to)

    def share(q, offset, sign):
        to = torus.peer(pos, core, offset, sign)
        slot = my_et if sign > 0 else to["et"]
        return remote(gate_in, gate_all.at[slot], h_send.at[q], h_recv.at[q], to)

    for q, offset in enumerate(torus.peers()):
        hand(q, offset, 1).start()
    for q, offset in enumerate(torus.experts()):
        p, k = torus.other_expert(pos, core, offset, 1)
        to = torus.device(p, k)
        remote(sel.at[to["exp"]], gate_in.at[me], g_send.at[q], g_recv.at[q], to).start()
    gate_in[me] = sel[me]
    inbox[my_et] = packed[my_et]
    for q, offset in enumerate(torus.peers()):
        hand(q, offset, -1).wait_recv()
    count = packed.shape[1]
    for i in range(packed.shape[0]):
        stack[i * count:(i + 1) * count, :] = inbox[i].astype(F32)
    for d in range(2):
        for o in range(NS // 2):
            blk[d, o] = stack[o * ROWS:(o + 1) * ROWS, d * width:(d + 1) * width].astype(BF16)

    def region(s, phase, shift, part=None, c=core):
        order = ORDERS[s // 2]
        at = dict(pos)
        for axis in order[:phase]:
            at[axis] = None
        if phase < 3:
            at[order[phase]] = torus.shift(pos, order[phase], shift)
        zl, zh, y, col = chosen_part(torus, at, part, width)
        return out.at[zl, s % 2, zh, y, c, s // 2, :, col]

    def reach(s):
        n = torus.n[ORDERS[s // 2][0]]
        up = n // 2 if s % 2 == 0 else n - 1 - n // 2
        return up, n - 1 - up

    def first(s, d, hop):
        i = hop - 1 if d > 0 else reach(s)[0] + hop - 1
        here = region(s, 0, -d * (hop - 1))
        src = blk.at[s % 2, s // 2] if hop == 1 else here
        return remote(src, here, p1_send.at[s, i], p1_recv.at[s, i],
                      torus.device(torus.moved(pos, ORDERS[s // 2][0], d), core))

    def first_landed(s, d, hop):
        i = hop - 1 if d > 0 else reach(s)[0] + hop - 1
        here = region(s, 0, -d * hop)
        return remote(here, here, p1_send.at[s, i], p1_recv.at[s, i], sibling)

    def chain(s):
        up, down = reach(s)
        return [(d, h) for h in range(1, max(up, down) + 1) for d in (1, -1) if h <= (up if d > 0 else down)]

    def ring(s, phase, k, part):
        d = 1 if s % 2 == 0 else -1
        here = region(s, phase, -d * k, part)
        i = phase - 1
        return remote(here, here, send.at[s, i, k, part], recv.at[s, i, k, part],
                      torus.device(torus.moved(pos, ORDERS[s // 2][phase], d), core))

    def landed(s, phase, k, part):
        d = 1 if s % 2 == 0 else -1
        here = region(s, phase, -d * (k + 1), part)
        return remote(here, here, send.at[s, phase - 1, k, part], recv.at[s, phase - 1, k, part], sibling)

    def across(s, src, dst):
        return remote(src, dst, sib_send.at[s], sib_recv.at[s], sibling)

    def own(s):
        return pltpu.make_async_copy(blk.at[s % 2, s // 2], region(s, 0, 0), loc.at[s])

    for s in range(NS):
        for d, h in chain(s):
            if h == 1:
                first(s, d, 1).start()
        own(s).start()
    for s in range(NS):
        own(s).wait()
    for hop in range(1, max(torus.n.values()) // 2 + 1):
        for s in range(NS):
            mine = [(d, h) for d, h in chain(s) if h == hop]
            for d, h in mine:
                first_landed(s, d, h).wait_recv()
                if (d, h + 1) in chain(s):
                    first(s, d, h + 1).start()
            if mine and hop == max(h for _, h in chain(s)):
                for part in range(2):
                    ring(s, 1, 0, part).start()
                whole = region(s, 1, 0)
                across(s, whole, whole).start()
    for q, offset in enumerate(torus.experts()):
        p, k = torus.other_expert(pos, core, offset, -1)
        came = torus.device(p, k)
        remote(sel.at[me], gate_in.at[came["exp"]], g_send.at[q], g_recv.at[q], came).wait_recv()
    for q, offset in enumerate(torus.peers()):
        share(q, offset, 1).start()
    gate_all[my_et] = gate_in[...]
    events = []
    for s in range(NS):
        order = ORDERS[s // 2]
        at = 0.0
        for phase in (1, 2):
            w = volume(torus, order[:phase]) * (1.5 if phase == 1 else 1.0)
            for k in range(torus.n[order[phase]] - 1):
                for part in range(2):
                    at += w / 2 + 0.5
                    events.append((at, s, phase, k, part))
            at += 1.0
    for _, s, phase, k, part in sorted(events):
        order = ORDERS[s // 2]
        arrived = landed(s, phase, k, part)
        arrived.wait_recv()
        if k + 1 < torus.n[order[phase]] - 1:
            ring(s, phase, k + 1, part).start()
        elif phase == 1 and part == 1:
            for half in range(2):
                ring(s, 2, 0, half).start()
        d = 1 if s % 2 == 0 else -1
        here = region(s, phase, -d * (k + 1), part)
        across(s, here, here).start()
    for q, offset in enumerate(torus.peers()):
        share(q, offset, -1).wait_recv()
    gate_out[...] = gate_all[...]
    for q, offset in enumerate(torus.peers()):
        share(q, offset, 1).wait_send()
        hand(q, offset, 1).wait_send()
    for s in range(NS):
        order = ORDERS[s // 2]
        for d, h in chain(s):
            first(s, d, h).wait_send()
        for phase in (1, 2):
            for k in range(torus.n[order[phase]] - 1):
                for part in range(2):
                    ring(s, phase, k, part).wait_send()
        whole, other = region(s, 3, 0), region(s, 3, 0, None, 1 - core)
        across(s, whole, whole).wait_send()
        across(s, other, other).wait_recv()
    for q, offset in enumerate(torus.experts()):
        p, k = torus.other_expert(pos, core, offset, 1)
        to = torus.device(p, k)
        remote(sel.at[to["exp"]], gate_in.at[me], g_send.at[q], g_recv.at[q], to).wait_send()


def gather_all(torus, packed, sel):
    width = packed.shape[2] // 2
    n = torus.n
    shape = (torus.nzl, 2, torus.nzh, n["y"], 2, NS // 2, ROWS, n["x"] * width)
    most = max(n.values()) - 1
    others, peers = len(torus.experts()), len(torus.peers())
    gates = (packed.shape[0],) + sel.shape
    dma = pltpu.SemaphoreType.DMA
    vm = pltpu.VMEM
    return pl.pallas_call(
        functools.partial(gather_kernel, torus, width),
        out_shape=[jax.ShapeDtypeStruct(shape, packed.dtype), jax.ShapeDtypeStruct(gates, sel.dtype)],
        in_specs=[pl.BlockSpec(memory_space=pltpu.VMEM)] * 2,
        out_specs=[pl.BlockSpec(memory_space=pl.ANY), pl.BlockSpec(memory_space=pltpu.VMEM)],
        scratch_shapes=[vm(sel.shape, sel.dtype), vm(gates, sel.dtype), vm(packed.shape, packed.dtype),
                        vm((NS * OCT, 2 * width), F32), vm((2, NS // 2, ROWS, width), packed.dtype),
                        dma((NS,)), dma((NS, most)), dma((NS, most)),
                        dma((NS, 2, most, 2)), dma((NS, 2, most, 2)), dma((NS,)), dma((NS,)),
                        dma((others,)), dma((others,)), dma((peers,)), dma((peers,)), dma((peers,)), dma((peers,))],
        compiler_params=pltpu.CompilerParams(collective_id=0, has_side_effects=True),
        name="gather_all",
    )(packed, sel)


BACK = tuple(tuple(reversed(o)) for o in ORDERS)


def back_kernel(torus, depth, tile_cols, every, gates, wg, wu, wd, out, score_out, dg, du, dd,
                part, theirs, wcat, wdown, gt, wt, score, score_in, score_all, fin, ship, inbox, b0, b1, b2, b3, b4, b5, b6, b7, b8,
                w_sem, sib_send, sib_recv, send, recv, p3_send, p3_recv, s_send, s_recv, e_send, e_recv, h_send, h_recv):
    bufs = (b0, b1, b2, b3, b4, b5, b6, b7, b8)
    n = torus.n
    width = depth // (torus.nzl * n["x"])
    wide = n["x"] * width
    pos, core = torus.here()
    me = torus.device(pos, core)["exp"]
    my_et = torus.device(pos, core)["et"]
    sibling = torus.device(pos, 1 - core)
    hz = torus.nzh // 2
    group = hz * n["y"] * 2
    rows = group * ROWS
    tiles = NS
    half = depth // 2

    loads = [pltpu.make_async_copy(wg, wcat.at[:, pl.ds(0, LANE)], w_sem.at[0]),
             pltpu.make_async_copy(wu, wcat.at[:, pl.ds(LANE, LANE)], w_sem.at[1]),
             pltpu.make_async_copy(wd, wdown, w_sem.at[2])]
    for c in loads:
        c.start()

    def block(at, s, k=core):
        zl, zh, y, col = chosen_part(torus, at, None, width)
        return part.at[k, zl, zh, y, s, :, col]

    def place(s, phase, shift):
        order = BACK[s // 2]
        at = dict(pos)
        for axis in order[phase + 1:]:
            at[axis] = None
        at[order[phase]] = torus.shift(pos, order[phase], shift)
        return at

    def piece(at, s, h):
        zl, zh, y, col = chosen_part(torus, at, h, width)
        return part.at[core, zl, zh, y, s, :, col]

    def slot(s, phase, k, h):
        ref = bufs[s // 2 * 3 + phase].at[s % 2, k]
        if h is None:
            return ref
        order = BACK[s // 2]
        if "z" in order[phase + 1:]:
            return ref.at[h]
        if "y" in order[phase + 1:]:
            return ref.at[pl.ds(h * (n["y"] // 2), n["y"] // 2)]
        return ref.at[:, pl.ds(h * (n["x"] // 2) * width, n["x"] // 2 * width)]

    def ring(s, phase, k, h):
        d = 1 if s % 2 == 0 else -1
        return remote(piece(place(s, phase, -d * (k + 1)), s, h), slot(s, phase, k, h),
                      send.at[s, phase, k, h], recv.at[s, phase, k, h],
                      torus.device(torus.moved(pos, BACK[s // 2][phase], d), core))

    def last(s, by):
        axis = BACK[s // 2][2]
        return remote(block(place(s, 2, by), s), bufs[s // 2 * 3 + 2].at[s % 2, by - 1],
                      p3_send.at[s, by - 1], p3_recv.at[s, by - 1],
                      torus.device(torus.moved(pos, axis, by), core))

    def add(s, at, got, h):
        zl0, zh0, y0, col0 = None, None, None, None
        nzl, nzh, ny = 1, 1, 1
        zbase = ybase = 0
        if at["z"] is None:
            nzh = torus.nzh
            nzl = torus.nzl if h is None else 1
            zbase = 0 if h is None else h
        else:
            zl0, zh0 = torus.split(at["z"])
        if at["y"] is None:
            ny = n["y"]
            if h is not None and at["z"] is not None:
                ny, ybase = n["y"] // 2, h * (n["y"] // 2)
        else:
            y0 = at["y"]
        if at["x"] is None:
            cols = wide
            col0 = pl.ds(0, wide)
            if h is not None and at["z"] is not None and at["y"] is not None:
                cols = wide // 2
                col0 = pl.ds(h * cols, cols)
        else:
            cols = width
            col0 = pl.ds(pl.multiple_of(at["x"] * width, LANE), width)

        def one(i, carry):
            iy = lax.rem(i, ny)
            iz = lax.div(i, ny)
            izh = lax.rem(iz, nzh)
            izl = lax.div(iz, nzh)
            where = ()
            if at["z"] is None:
                where = (izh,) if h is not None else (izl, izh)
                zl, zh = izl + zbase, izh
            else:
                zl, zh = zl0, zh0
            if at["y"] is None:
                where = where + (iy,)
                y = iy + ybase
            else:
                y = y0
            part[core, zl, zh, y, s, :, col0] += got[where + (slice(None), slice(None))]
            return carry

        lax.fori_loop(0, nzl * nzh * ny, one, 0)

    def cross(t):
        o, hh = t // 2, t % 2
        zs, os = pl.ds(hh * hz, hz), pl.ds(2 * o, 2)
        return remote(part.at[1 - core, :, zs, :, os], theirs.at[:, zs, :, os], sib_send.at[t], sib_recv.at[t], sibling)

    everywhere = {"x": None, "y": None, "z": None}

    def begin(o):
        for t in (2 * o, 2 * o + 1):
            cross(t).wait_recv()
        for s in (2 * o, 2 * o + 1):
            add(s, everywhere, theirs.at[:, :, :, s], None)
            for h in range(2):
                ring(s, 0, 0, h).start()

    def rows_phase(xs, ds, x_sem, d_sem):
        def fetch(which, t):
            o, hh = t // 2, t % 2
            buf, sem = (xs, x_sem) if which == 0 else (ds, d_sem)
            return [pltpu.make_async_copy(every.at[which, d, pl.ds(hh * hz, hz), :, :, o], buf.at[d], sem.at[d])
                    for d in range(2)]

        for which in range(2):
            for c in fetch(which, 0):
                c.start()
        score[...] = jnp.zeros_like(score)
        torus.greet(pos, core)
        for c in loads:
            c.wait()
        for t in range(tiles):
            o, hh = t // 2, t % 2
            for c in fetch(0, t):
                c.wait()
            pre = jnp.dot(xs[0].reshape(rows, half), wcat[:half, :], preferred_element_type=F32)
            pre = pre + jnp.dot(xs[1].reshape(rows, half), wcat[half:, :], preferred_element_type=F32)
            if t + 1 < tiles:
                for c in fetch(0, t + 1):
                    c.start()
            for c in fetch(1, t):
                c.wait()
            back = lax.dot_general(ds[0].reshape(rows, half), wdown[:, :half], NT, preferred_element_type=F32)
            back = back + lax.dot_general(ds[1].reshape(rows, half), wdown[:, half:], NT, preferred_element_type=F32)
            if t + 1 < tiles:
                for c in fetch(1, t + 1):
                    c.start()
            gate_pre, up_pre = pre[:, :LANE], pre[:, LANE:]
            scale = gates[t]
            sigma = jax.nn.sigmoid(gate_pre)
            silu = gate_pre * sigma
            act = silu * up_pre
            dact = scale * back
            grad_gate = dact * up_pre * sigma * (1.0 + gate_pre * (1.0 - sigma))
            grad_up = dact * silu
            cols = pl.ds(t * rows, rows)
            gt[:LANE, cols] = grad_gate.T.astype(BF16)
            gt[LANE:, cols] = grad_up.T.astype(BF16)
            wt[:, cols] = (scale * act).T.astype(BF16)
            sums = jnp.sum((act * back).T, axis=0, keepdims=True)
            for g in range(group):
                score[hh * group + g, :, o * ROWS:(o + 1) * ROWS] = sums[:, g * ROWS:(g + 1) * ROWS]
            both = jnp.concatenate([grad_gate.astype(BF16), grad_up.astype(BF16)], axis=1)
            for j in range(torus.nzl * n["x"]):
                zl, x = j // n["x"], j % n["x"]
                grad = lax.dot_general(both, wcat[j * width:(j + 1) * width, :], NT, preferred_element_type=F32)
                grad = grad.reshape(hz, n["y"], 2, 2, OCT, width).astype(BF16)
                for k in range(2):
                    part[k, zl, hh * hz:(hh + 1) * hz, :, 2 * o:2 * o + 2, :, x * width:(x + 1) * width] = grad[:, :, k]
            cross(t).start()
            if t in (2, 4):
                begin(t // 2 - 1)

    pl.run_scoped(
        rows_phase,
        pltpu.VMEM((2, hz, n["y"], 2, ROWS, half), BF16), pltpu.VMEM((2, hz, n["y"], 2, ROWS, half), BF16),
        pltpu.SemaphoreType.DMA((2,)), pltpu.SemaphoreType.DMA((2,)))

    def message(q, offset, sign):
        p, k = torus.other_expert(pos, core, offset, sign)
        other = torus.device(p, k)
        return remote(score.at[other["exp"]], score_in.at[me if sign > 0 else other["exp"]],
                      s_send.at[q], s_recv.at[q], other)

    def share(q, offset, sign):
        to = torus.peer(pos, core, offset, sign)
        slot = my_et if sign > 0 else to["et"]
        return remote(score_in, score_all.at[slot], h_send.at[q], h_recv.at[q], to)

    def hand(q, offset, sign):
        to = torus.peer(pos, core, offset, sign)
        slot = my_et if sign > 0 else to["et"]
        return remote(ship.at[to["et"]], inbox.at[slot], e_send.at[q], e_recv.at[q], to)

    for q, offset in enumerate(torus.experts()):
        message(q, offset, 1).start()
    score_in[me] = score[me]

    def exchange(xt, dt, sg, su, sd, x_sem, d_sem, o_sem):
        units = depth // tile_cols
        per = half // tile_cols

        def fetch(u, which):
            buf, sem = (xt, x_sem) if which == 0 else (dt, d_sem)
            d, c = u // per, pl.ds(u % per * tile_cols, tile_cols)
            return [pltpu.make_async_copy(every.at[which, d, pl.ds(t % 2 * hz, hz), :, :, t // 2, :, c],
                                          buf.at[u % 2, t], sem.at[u % 2, t]) for t in range(tiles)]

        def put(u):
            c = pl.ds(u * tile_cols, tile_cols)
            return [pltpu.make_async_copy(sg.at[u % 2], dg.at[c], o_sem.at[u % 2, 0]),
                    pltpu.make_async_copy(su.at[u % 2], du.at[c], o_sem.at[u % 2, 1]),
                    pltpu.make_async_copy(sd.at[u % 2], dd.at[:, c], o_sem.at[u % 2, 2])]

        def get(u):
            for which in range(2):
                for c in fetch(u, which):
                    c.start()

        def unit(u):
            if u + 1 < units:
                get(u + 1)
            for which in range(2):
                for c in fetch(u, which):
                    c.wait()
            if u >= 2:
                for c in put(u - 2):
                    c.wait()
            both = jnp.dot(gt[...], xt[u % 2].reshape(tiles * rows, tile_cols), preferred_element_type=F32).T
            sg[u % 2] = both[:, :LANE].astype(BF16)
            su[u % 2] = both[:, LANE:].astype(BF16)
            down = jnp.dot(wt[...], dt[u % 2].reshape(tiles * rows, tile_cols), preferred_element_type=F32)
            sd[u % 2] = down.astype(BF16)
            for c in put(u):
                c.start()

        get(0)
        begin(2)
        events = []
        for s in range(NS):
            order = BACK[s // 2]
            at = (s // 2) * 3.0
            for phase in (0, 1):
                w = volume(torus, order[phase + 1:])
                for k in range(n[order[phase]] - 1):
                    for h in range(2):
                        at += w / 2 + 0.5
                        events.append((at, s, phase, k, h))
                at += 2.0
            events.append((at + 6.0, s, 2, 0, 0))
        events.sort()
        done = 0
        for i, (_, s, phase, k, h) in enumerate(events):
            if i == 4:
                for q, offset in enumerate(torus.experts()):
                    message(q, offset, -1).wait_recv()
                for q, offset in enumerate(torus.peers()):
                    share(q, offset, 1).start()
                score_all[my_et] = score_in[...]
            while done < units and done * len(events) * 3 // 5 <= i * units:
                unit(done)
                done += 1
            order = BACK[s // 2]
            d = 1 if s % 2 == 0 else -1
            if phase < 2:
                ring(s, phase, k, h).wait_recv()
                add(s, place(s, phase, -d * (k + 2)), slot(s, phase, k, h), h)
                if k + 1 < n[order[phase]] - 1:
                    ring(s, phase, k + 1, h).start()
                elif h == 1 and phase == 0:
                    for hh in range(2):
                        ring(s, 1, 0, hh).start()
                elif h == 1:
                    for by in range(1, n[order[2]]):
                        last(s, by).start()
            else:
                zl, zh = torus.split(pos["z"])
                col = pl.ds(pl.multiple_of(pos["x"] * width, LANE), width)
                total = part[core, zl, zh, pos["y"], s, :, col].astype(F32)
                for by in range(1, n[order[2]]):
                    last(s, by).wait_recv()
                    total = total + bufs[s // 2 * 3 + 2][s % 2, by - 1].astype(F32)
                fin[s * OCT:(s + 1) * OCT, :] = total
        count = out.shape[1]
        for i in range(out.shape[0]):
            ship[i] = fin[i * count:(i + 1) * count, :].astype(BF16)
        for q, offset in enumerate(torus.peers()):
            hand(q, offset, 1).start()
        inbox[my_et] = ship[my_et]
        while done < units:
            unit(done)
            done += 1
        for u in (units - 2, units - 1):
            for c in put(u):
                c.wait()

    stage = pltpu.VMEM((2, tile_cols, LANE), BF16)
    tiled = pltpu.VMEM((2, tiles, hz, n["y"], 2, ROWS, tile_cols), BF16)
    dma = pltpu.SemaphoreType.DMA
    pl.run_scoped(exchange, tiled, tiled, stage, stage, pltpu.VMEM((2, LANE, tile_cols), BF16),
                  dma((2, tiles)), dma((2, tiles)), dma((2, 3)))

    for q, offset in enumerate(torus.peers()):
        hand(q, offset, -1).wait_recv()
        share(q, offset, -1).wait_recv()
    out[...] = inbox[...]
    score_out[...] = score_all[...]
    for q, offset in enumerate(torus.peers()):
        hand(q, offset, 1).wait_send()
        share(q, offset, 1).wait_send()
    for q, offset in enumerate(torus.experts()):
        message(q, offset, 1).wait_send()
    for t in range(tiles):
        cross(t).wait_send()
    for s in range(NS):
        order = BACK[s // 2]
        for phase in (0, 1):
            for k in range(n[order[phase]] - 1):
                for h in range(2):
                    ring(s, phase, k, h).wait_send()
        for by in range(1, n[order[2]]):
            last(s, by).wait_send()


def back_all(torus, every, gates, wg, wu, wd):
    n = torus.n
    depth = wg.shape[0]
    width = depth // (torus.nzl * n["x"])
    wide = n["x"] * width
    experts = torus.nzh * n["y"] * 2
    bufs = []
    for order in BACK:
        for phase, axis in enumerate(order):
            free = order[phase + 1:]
            shape = (2, n[axis] - 1)
            if "z" in free:
                shape += (torus.nzl, torus.nzh)
            if "y" in free:
                shape += (n["y"],)
            shape += (OCT, wide if "x" in free else width)
            bufs.append(pltpu.VMEM(shape, BF16))
    most = max(n.values()) - 1
    others, peers = len(torus.experts()), len(torus.peers())
    n_et = peers + 1
    total = experts * NS * OCT
    owned = (n_et, NS * OCT // n_et, width)
    dma = pltpu.SemaphoreType.DMA
    vm = pltpu.VMEM
    half = (torus.nzl, torus.nzh, n["y"], NS, OCT, wide)
    any_ = pl.BlockSpec(memory_space=pl.ANY)
    vspec = pl.BlockSpec(memory_space=pltpu.VMEM)
    return pl.pallas_call(
        functools.partial(back_kernel, torus, depth, min(512, depth // 2)),
        out_shape=[jax.ShapeDtypeStruct(owned, BF16),
                   jax.ShapeDtypeStruct((n_et, experts, 1, LANE), F32),
                   jax.ShapeDtypeStruct((depth, LANE), BF16),
                   jax.ShapeDtypeStruct((depth, LANE), BF16),
                   jax.ShapeDtypeStruct((LANE, depth), BF16)],
        in_specs=[any_, vspec, any_, any_, any_],
        out_specs=[vspec, vspec, any_, any_, any_],
        scratch_shapes=[vm((2,) + half, BF16), vm(half, BF16), vm((depth, 2 * LANE), BF16), vm((LANE, depth), BF16),
                        vm((2 * LANE, total), BF16), vm((LANE, total), BF16), vm((experts, 1, LANE), F32),
                        vm((experts, 1, LANE), F32), vm((n_et, experts, 1, LANE), F32), vm((NS * OCT, width), F32),
                        vm(owned, BF16), vm(owned, BF16), *bufs, dma((3,)), dma((NS,)), dma((NS,)),
                        dma((NS, 2, most, 2)), dma((NS, 2, most, 2)), dma((NS, most)), dma((NS, most)),
                        dma((others,)), dma((others,)), dma((peers,)), dma((peers,)), dma((peers,)), dma((peers,))],
        compiler_params=pltpu.CompilerParams(
            collective_id=1, has_side_effects=True, vmem_limit_bytes=67043328),
        name="back_all",
    )(every, gates, wg, wu, wd)


def on_device(torus, tokens, grad_out, gates, expert_ids, gate_weight, up_weight, down_weight):
    count, depth = tokens.shape
    n = torus.n
    n_et = torus.nzl * n["x"]
    n_exp = torus.nzh * n["y"] * 2
    share = depth // (2 * n["x"])
    experts = jnp.arange(LANE, dtype=jnp.int32)
    chosen = expert_ids[:, :, None] == experts[None, None, :]
    table = jnp.sum(jnp.where(chosen, gates[:, :, None].astype(F32), 0.0), axis=1).astype(BF16)
    both = jnp.stack([tokens, grad_out], axis=0).reshape(2, count, 2, n["x"], share)
    packed = both.transpose(0, 3, 1, 2, 4).reshape(n_et, count, 2 * share)
    sel = jnp.pad(table.astype(F32).T[:n_exp], ((0, 0), (0, LANE - count)))[:, None, :]
    every, scale = gather_all(torus, packed, sel)
    rows = n_et * count
    scale = scale[:, :, 0, :count].transpose(1, 0, 2).reshape(2, n_exp // 2, NS // 2, ROWS).transpose(2, 0, 1, 3)
    scale = jnp.broadcast_to(scale.reshape(NS, n_exp // 2 * ROWS, 1), (NS, n_exp // 2 * ROWS, LANE))
    owned, score, dg, du, dd = back_all(torus, every, scale, gate_weight[0], up_weight[0], down_weight[0])
    input_grad = owned.transpose(1, 0, 2).reshape(count, depth)
    score = score[:, :, 0, :rows].reshape(n_et, n_exp, n_et, count)
    score = lax.dynamic_index_in_dim(score, lax.axis_index("et"), axis=2, keepdims=False)
    score = jnp.sum(score.astype(BF16).astype(F32), axis=0)
    chosen = chosen[:, :, :n_exp]
    gate_grad = jnp.sum(jnp.where(chosen, score.T[:, None, :], 0.0), axis=2)
    return input_grad, gate_grad, dg[None], du[None], dd[None]


def solution(mesh, dims=(4, 4, 4, 2)):
    placed = (
        P(("exp", "et"), None),
        P(("exp", "et"), None),
        P(("exp", "et"), None),
        P(("exp", "et"), None),
        P("exp", None, "et"),
        P("exp", None, "et"),
        P("exp", "et", None),
    )
    return jax.shard_map(
        functools.partial(on_device, Torus(*dims)),
        mesh=mesh,
        in_specs=placed,
        out_specs=(
            P(("exp", "et"), None),
            P(("exp", "et"), None),
            P("exp", None, "et"),
            P("exp", None, "et"),
            P("exp", "et", None),
        ),
        check_vma=False,
    )
```

```python
import functools
import jax
import jax.numpy as jnp
from jax import lax
from jax.experimental import pallas as pl
from jax.experimental.pallas import tpu as pltpu
from jax.sharding import PartitionSpec as P

TOP = 8
LANE = 128
NS = 6
OCT = 8
MESH = pl.DeviceIdType.MESH
ORDERS = (("x", "y", "z"), ("z", "y", "x"), ("z", "x", "y"))
ROWS = 16
NT = (((1,), (1,)), ((), ()))
F32 = jnp.float32
BF16 = jnp.bfloat16


class Torus:
    def __init__(self, nx, ny, nzh, nzl):
        self.n = {"x": nx, "y": ny, "z": nzh * nzl}
        self.nzh, self.nzl = nzh, nzl

    def here(self):
        e = lax.axis_index("exp")
        t = lax.axis_index("et")
        ny, nx = self.n["y"], self.n["x"]
        core = lax.rem(e, 2)
        y = lax.rem(lax.div(e, 2), ny)
        zh = lax.div(e, 2 * ny)
        x = lax.rem(t, nx)
        zl = lax.div(t, nx)
        return {"x": x, "y": y, "z": zh * self.nzl + zl}, core

    def split(self, z):
        return lax.rem(z, self.nzl), lax.div(z, self.nzl)

    def device(self, pos, core):
        zl, zh = self.split(pos["z"])
        return {
            "exp": (zh * self.n["y"] + pos["y"]) * 2 + core,
            "et": zl * self.n["x"] + pos["x"],
        }

    def shift(self, pos, axis, by):
        n = self.n[axis]
        return lax.rem(pos[axis] + (by % n + n), n)

    def moved(self, pos, axis, by):
        other = dict(pos)
        other[axis] = self.shift(pos, axis, by)
        return other

    def experts(self):
        return [(c, y, h) for c in range(2) for y in range(self.n["y"]) for h in range(self.nzh) if c or y or h]

    def other_expert(self, pos, core, offset, sign):
        c, y, h = offset
        out = self.moved(pos, "y", sign * y)
        out["z"] = self.shift(pos, "z", sign * h * self.nzl)
        return out, (1 - core if c else core)

    def peers(self):
        return [(l, x) for l in range(self.nzl) for x in range(self.n["x"]) if l or x]

    def peer(self, pos, core, offset, sign):
        l, x = offset
        out = self.moved(pos, "x", sign * x)
        zl, zh = self.split(pos["z"])
        out["z"] = zh * self.nzl + (lax.rem(zl + l, self.nzl) if l else zl)
        return self.device(out, core)

    def greet(self, pos, core):
        seen, partners = set(), []
        for c, y, h in self.experts():
            p, k = self.other_expert(pos, core, (c, y, h), 1)
            partners.append(self.device(p, k))
            if not c and not y:
                seen.add(("z", h * self.nzl))
            if not c and not h:
                seen.add(("y", y))
        for axis in "xyz":
            for by in range(1, self.n[axis]):
                if (axis, by) not in seen:
                    partners.append(self.device(self.moved(pos, axis, by), core))
        for l, x in self.peers():
            if l and x:
                partners.append(self.peer(pos, core, (l, x), 1))
        barrier = pltpu.get_barrier_semaphore()
        for p in partners:
            pl.semaphore_signal(barrier, inc=1, device_id=p, device_id_type=MESH)
        pl.semaphore_wait(barrier, len(partners))


def remote(src, dst, send, recv, device):
    return pltpu.make_async_remote_copy(
        src_ref=src, dst_ref=dst, send_sem=send, recv_sem=recv, device_id=device, device_id_type=MESH)


def chosen_part(torus, at, part, width):
    zl, zh, y = slice(None), slice(None), slice(None)
    if at["z"] is not None:
        zl, zh = torus.split(at["z"])
    if at["y"] is not None:
        y = at["y"]
    col = slice(None)
    if at["x"] is not None:
        col = pl.ds(pl.multiple_of(at["x"] * width, LANE), width)
    if part is not None:
        if at["z"] is None:
            zl = part
        elif at["y"] is None:
            n = torus.n["y"] // 2
            y = pl.ds(part * n, n)
        else:
            n = torus.n["x"] // 2 * width
            col = pl.ds(part * n, n)
    return zl, zh, y, col


def volume(torus, axes):
    w = 1
    for a in axes:
        w *= torus.n[a]
    return w


def gather_kernel(torus, width, packed, sel, out, gate_out, gate_in, gate_all, inbox, stack, blk, loc, p1_send, p1_recv,
                  send, recv, sib_send, sib_recv, g_send, g_recv, e_send, e_recv, h_send, h_recv):
    pos, core = torus.here()
    me = torus.device(pos, core)["exp"]
    my_et = torus.device(pos, core)["et"]
    sibling = torus.device(pos, 1 - core)
    torus.greet(pos, core)

    def hand(q, offset, sign):
        to = torus.peer(pos, core, offset, sign)
        slot = my_et if sign > 0 else to["et"]
        return remote(packed.at[to["et"]], inbox.at[slot], e_send.at[q], e_recv.at[q], to)

    def share(q, offset, sign):
        to = torus.peer(pos, core, offset, sign)
        slot = my_et if sign > 0 else to["et"]
        return remote(gate_in, gate_all.at[slot], h_send.at[q], h_recv.at[q], to)

    for q, offset in enumerate(torus.peers()):
        hand(q, offset, 1).start()
    for q, offset in enumerate(torus.experts()):
        p, k = torus.other_expert(pos, core, offset, 1)
        to = torus.device(p, k)
        remote(sel.at[to["exp"]], gate_in.at[me], g_send.at[q], g_recv.at[q], to).start()
    gate_in[me] = sel[me]
    inbox[my_et] = packed[my_et]
    for q, offset in enumerate(torus.peers()):
        hand(q, offset, -1).wait_recv()
    count = packed.shape[1]
    for i in range(packed.shape[0]):
        stack[i * count:(i + 1) * count, :] = inbox[i].astype(F32)
    for d in range(2):
        for o in range(NS // 2):
            blk[d, o] = stack[o * ROWS:(o + 1) * ROWS, d * width:(d + 1) * width].astype(BF16)

    def region(s, phase, shift, part=None, c=core):
        order = ORDERS[s // 2]
        at = dict(pos)
        for axis in order[:phase]:
            at[axis] = None
        if phase < 3:
            at[order[phase]] = torus.shift(pos, order[phase], shift)
        zl, zh, y, col = chosen_part(torus, at, part, width)
        return out.at[zl, s % 2, zh, y, c, s // 2, :, col]

    def reach(s):
        n = torus.n[ORDERS[s // 2][0]]
        up = n // 2 if s % 2 == 0 else n - 1 - n // 2
        return up, n - 1 - up

    def first(s, d, hop):
        i = hop - 1 if d > 0 else reach(s)[0] + hop - 1
        here = region(s, 0, -d * (hop - 1))
        src = blk.at[s % 2, s // 2] if hop == 1 else here
        return remote(src, here, p1_send.at[s, i], p1_recv.at[s, i],
                      torus.device(torus.moved(pos, ORDERS[s // 2][0], d), core))

    def first_landed(s, d, hop):
        i = hop - 1 if d > 0 else reach(s)[0] + hop - 1
        here = region(s, 0, -d * hop)
        return remote(here, here, p1_send.at[s, i], p1_recv.at[s, i], sibling)

    def chain(s):
        up, down = reach(s)
        return [(d, h) for h in range(1, max(up, down) + 1) for d in (1, -1) if h <= (up if d > 0 else down)]

    def stretch(s, phase, shift, part):
        d = 1 if s % 2 == 0 else -1
        if phase == 1:
            return region(s, 1, shift, part)
        order = ORDERS[s // 2]
        at = dict(pos)
        at[order[0]] = None
        at[order[1]] = torus.shift(pos, order[1], -d * part)
        at[order[2]] = torus.shift(pos, order[2], shift)
        zl, zh, y, col = chosen_part(torus, at, None, width)
        return out.at[zl, s % 2, zh, y, core, s // 2, :, col]

    def ring(s, phase, k, part):
        d = 1 if s % 2 == 0 else -1
        here = stretch(s, phase, -d * k, part)
        i = phase - 1
        return remote(here, here, send.at[s, i, k, part], recv.at[s, i, k, part],
                      torus.device(torus.moved(pos, ORDERS[s // 2][phase], d), core))

    def landed(s, phase, k, part):
        d = 1 if s % 2 == 0 else -1
        here = stretch(s, phase, -d * (k + 1), part)
        return remote(here, here, send.at[s, phase - 1, k, part], recv.at[s, phase - 1, k, part], sibling)

    def parts(s, phase):
        return 2 if phase == 1 else torus.n[ORDERS[s // 2][1]]

    def across(s, src, dst):
        return remote(src, dst, sib_send.at[s], sib_recv.at[s], sibling)

    def own(s):
        return pltpu.make_async_copy(blk.at[s % 2, s // 2], region(s, 0, 0), loc.at[s])

    for s in range(NS):
        for d, h in chain(s):
            if h == 1:
                first(s, d, 1).start()
        own(s).start()
    for s in range(NS):
        own(s).wait()
    for hop in range(1, max(torus.n.values()) // 2 + 1):
        for s in range(NS):
            mine = [(d, h) for d, h in chain(s) if h == hop]
            for d, h in mine:
                first_landed(s, d, h).wait_recv()
                if (d, h + 1) in chain(s):
                    first(s, d, h + 1).start()
            if mine and hop == max(h for _, h in chain(s)):
                for part in range(2):
                    ring(s, 1, 0, part).start()
                ring(s, 2, 0, 0).start()
                whole = region(s, 1, 0)
                across(s, whole, whole).start()
    for q, offset in enumerate(torus.experts()):
        p, k = torus.other_expert(pos, core, offset, -1)
        came = torus.device(p, k)
        remote(sel.at[me], gate_in.at[came["exp"]], g_send.at[q], g_recv.at[q], came).wait_recv()
    for q, offset in enumerate(torus.peers()):
        share(q, offset, 1).start()
    gate_all[my_et] = gate_in[...]
    events = []
    for s in range(NS):
        order = ORDERS[s // 2]
        base = volume(torus, order[:1]) * 0.7
        at = ready = 3.0 if order[0] == "x" else 12.0
        when = [at]
        for k in range(torus.n[order[1]] - 1):
            for part in range(2):
                at += base / 2 * 1.3 + 0.7
                events.append((at, s, 1, k, part))
            when.append(at)
        at = ready
        for k in range(torus.n[order[2]] - 1):
            later = []
            for part in range(torus.n[order[1]]):
                at = max(at, when[part] + 1.5) + base
                events.append((at, s, 2, k, part))
                later.append(at)
            when = later
    for _, s, phase, k, part in sorted(events):
        order = ORDERS[s // 2]
        landed(s, phase, k, part).wait_recv()
        if k + 1 < torus.n[order[phase]] - 1:
            ring(s, phase, k + 1, part).start()
        if phase == 1 and part == 1:
            ring(s, 2, 0, k + 1).start()
        d = 1 if s % 2 == 0 else -1
        here = stretch(s, phase, -d * (k + 1), part)
        across(s, here, here).start()
    for q, offset in enumerate(torus.peers()):
        share(q, offset, -1).wait_recv()
    gate_out[...] = gate_all[...]
    for q, offset in enumerate(torus.peers()):
        share(q, offset, 1).wait_send()
        hand(q, offset, 1).wait_send()
    for s in range(NS):
        order = ORDERS[s // 2]
        for d, h in chain(s):
            first(s, d, h).wait_send()
        for phase in (1, 2):
            for k in range(torus.n[order[phase]] - 1):
                for part in range(parts(s, phase)):
                    ring(s, phase, k, part).wait_send()
        whole, other = region(s, 3, 0), region(s, 3, 0, None, 1 - core)
        across(s, whole, whole).wait_send()
        across(s, other, other).wait_recv()
    for q, offset in enumerate(torus.experts()):
        p, k = torus.other_expert(pos, core, offset, 1)
        to = torus.device(p, k)
        remote(sel.at[to["exp"]], gate_in.at[me], g_send.at[q], g_recv.at[q], to).wait_send()


def gather_all(torus, packed, sel):
    width = packed.shape[2] // 2
    n = torus.n
    shape = (torus.nzl, 2, torus.nzh, n["y"], 2, NS // 2, ROWS, n["x"] * width)
    most = max(n.values()) - 1
    others, peers = len(torus.experts()), len(torus.peers())
    gates = (packed.shape[0],) + sel.shape
    dma = pltpu.SemaphoreType.DMA
    vm = pltpu.VMEM
    return pl.pallas_call(
        functools.partial(gather_kernel, torus, width),
        out_shape=[jax.ShapeDtypeStruct(shape, packed.dtype), jax.ShapeDtypeStruct(gates, sel.dtype)],
        in_specs=[pl.BlockSpec(memory_space=pltpu.VMEM)] * 2,
        out_specs=[pl.BlockSpec(memory_space=pl.ANY), pl.BlockSpec(memory_space=pltpu.VMEM)],
        scratch_shapes=[vm(sel.shape, sel.dtype), vm(gates, sel.dtype), vm(packed.shape, packed.dtype),
                        vm((NS * OCT, 2 * width), F32), vm((2, NS // 2, ROWS, width), packed.dtype),
                        dma((NS,)), dma((NS, most)), dma((NS, most)),
                        dma((NS, 2, most, 4)), dma((NS, 2, most, 4)), dma((NS,)), dma((NS,)),
                        dma((others,)), dma((others,)), dma((peers,)), dma((peers,)), dma((peers,)), dma((peers,))],
        compiler_params=pltpu.CompilerParams(collective_id=0, has_side_effects=True),
        name="gather_all",
    )(packed, sel)


BACK = tuple(tuple(reversed(o)) for o in ORDERS)


def back_kernel(torus, depth, tile_cols, every, gates, wg, wu, wd, out, score_out, dg, du, dd,
                part, theirs, wcat, wdown, gt, wt, score, score_in, score_all, fin, ship, inbox, b0, b1, b2, b3, b4, b5, b6, b7, b8,
                w_sem, sib_send, sib_recv, send, recv, p3_send, p3_recv, s_send, s_recv, e_send, e_recv, h_send, h_recv):
    bufs = (b0, b1, b2, b3, b4, b5, b6, b7, b8)
    n = torus.n
    width = depth // (torus.nzl * n["x"])
    wide = n["x"] * width
    pos, core = torus.here()
    me = torus.device(pos, core)["exp"]
    my_et = torus.device(pos, core)["et"]
    sibling = torus.device(pos, 1 - core)
    hz = torus.nzh // 2
    group = hz * n["y"] * 2
    rows = group * ROWS
    tiles = NS
    half = depth // 2

    loads = [pltpu.make_async_copy(wg, wcat.at[:, pl.ds(0, LANE)], w_sem.at[0]),
             pltpu.make_async_copy(wu, wcat.at[:, pl.ds(LANE, LANE)], w_sem.at[1]),
             pltpu.make_async_copy(wd, wdown, w_sem.at[2])]
    for c in loads:
        c.start()

    def block(at, s, k=core):
        zl, zh, y, col = chosen_part(torus, at, None, width)
        return part.at[k, zl, zh, y, s, :, col]

    def place(s, phase, shift):
        order = BACK[s // 2]
        at = dict(pos)
        for axis in order[phase + 1:]:
            at[axis] = None
        at[order[phase]] = torus.shift(pos, order[phase], shift)
        return at

    def spot(s, phase, shift, q):
        at = place(s, phase, shift)
        if phase == 0:
            d = 1 if s % 2 == 0 else -1
            at[BACK[s // 2][1]] = torus.shift(pos, BACK[s // 2][1], -d * (q + 1))
        return at

    def slot(s, phase, k, q):
        ref = bufs[s // 2 * 3 + phase]
        return ref.at[s % 2, k, q] if phase == 0 else ref.at[s % 2, k]

    def ring(s, phase, k, q):
        d = 1 if s % 2 == 0 else -1
        return remote(block(spot(s, phase, -d * (k + 1), q), s), slot(s, phase, k, q),
                      send.at[s, phase, k, q], recv.at[s, phase, k, q],
                      torus.device(torus.moved(pos, BACK[s // 2][phase], d), core))

    def last(s, by):
        axis = BACK[s // 2][2]
        return remote(block(place(s, 2, by), s), bufs[s // 2 * 3 + 2].at[s % 2, by - 1],
                      p3_send.at[s, by - 1], p3_recv.at[s, by - 1],
                      torus.device(torus.moved(pos, axis, by), core))

    def add(s, at, got, h):
        zl0, zh0, y0, col0 = None, None, None, None
        nzl, nzh, ny = 1, 1, 1
        zbase = ybase = 0
        if at["z"] is None:
            nzh = torus.nzh
            nzl = torus.nzl if h is None else 1
            zbase = 0 if h is None else h
        else:
            zl0, zh0 = torus.split(at["z"])
        if at["y"] is None:
            ny = n["y"]
            if h is not None and at["z"] is not None:
                ny, ybase = n["y"] // 2, h * (n["y"] // 2)
        else:
            y0 = at["y"]
        if at["x"] is None:
            cols = wide
            col0 = pl.ds(0, wide)
            if h is not None and at["z"] is not None and at["y"] is not None:
                cols = wide // 2
                col0 = pl.ds(h * cols, cols)
        else:
            cols = width
            col0 = pl.ds(pl.multiple_of(at["x"] * width, LANE), width)

        def one(i, carry):
            iy = lax.rem(i, ny)
            iz = lax.div(i, ny)
            izh = lax.rem(iz, nzh)
            izl = lax.div(iz, nzh)
            where = ()
            if at["z"] is None:
                where = (izh,) if h is not None else (izl, izh)
                zl, zh = izl + zbase, izh
            else:
                zl, zh = zl0, zh0
            if at["y"] is None:
                where = where + (iy,)
                y = iy + ybase
            else:
                y = y0
            part[core, zl, zh, y, s, :, col0] += got[where + (slice(None), slice(None))]
            return carry

        lax.fori_loop(0, nzl * nzh * ny, one, 0)

    def cross(o, hh):
        t = 2 * o + hh
        zs, os = pl.ds(hh * hz, hz), pl.ds(2 * o, 2)
        return remote(part.at[1 - core, :, zs, :, os], theirs.at[:, zs, :, os], sib_send.at[t], sib_recv.at[t], sibling)

    everywhere = {"x": None, "y": None, "z": None}

    def begin(o):
        for hh in range(2):
            cross(o, hh).wait_recv()
        for s in (2 * o, 2 * o + 1):
            add(s, everywhere, theirs.at[:, :, :, s], None)
            for q in range(n[BACK[s // 2][1]]):
                ring(s, 0, 0, q).start()

    begun, past, sent = [], set(), set()

    def events():
        out = []
        for s in range(NS):
            o = s // 2
            a, b, c = (n[x] for x in BACK[o])
            size = volume(torus, BACK[o][2:]) * 0.35
            at = (19.0, 31.0, 42.0)[o]
            when = [at] * b
            for k in range(a - 1):
                for q in range(b):
                    at = max(at, when[q] + 2.0) + size
                    when[q] = at
                    out.append((at, s, 0, k, q))
            at = 0.0
            for k in range(b - 1):
                at = max(at, when[k]) + size + 2.0
                out.append((at, s, 1, k, 0))
            out.append((max(at, when[b - 1]) + 6.0, s, 2, 0, 0))
        return sorted(out)

    def handle(event):
        _, s, phase, k, q = event
        order = BACK[s // 2]
        a, b, c = (n[x] for x in order)
        d = 1 if s % 2 == 0 else -1
        if phase < 2:
            ring(s, phase, k, q).wait_recv()
            add(s, spot(s, phase, -d * (k + 2), q), slot(s, phase, k, q), None)
            if phase == 0 and k + 1 < a - 1:
                ring(s, 0, k + 1, q).start()
        else:
            zl, zh = torus.split(pos["z"])
            col = pl.ds(pl.multiple_of(pos["x"] * width, LANE), width)
            total = part[core, zl, zh, pos["y"], s, :, col].astype(F32)
            for by in range(1, c):
                last(s, by).wait_recv()
                total = total + bufs[s // 2 * 3 + 2][s % 2, by - 1].astype(F32)
            fin[s * OCT:(s + 1) * OCT, :] = total
        past.add((s, phase, k, q))
        for j in range(b):
            ready = (s, 0, a - 2, j) in past and (j == 0 or (s, 1, j - 1, 0) in past)
            if ready and (s, j) not in sent:
                sent.add((s, j))
                if j < b - 1:
                    ring(s, 1, j, 0).start()
                else:
                    for by in range(1, c):
                        last(s, by).start()

    todo = events()

    def rows_phase(xs, ds, x_sem, d_sem):
        def fetch(which, o, hh):
            buf, sem = (xs, x_sem) if which == 0 else (ds, d_sem)
            return [pltpu.make_async_copy(every.at[which, d, pl.ds(hh * hz, hz), :, :, o], buf.at[d], sem.at[d])
                    for d in range(2)]

        for which in range(2):
            for c in fetch(which, 0, 0):
                c.start()
        score[...] = jnp.zeros_like(score)
        torus.greet(pos, core)
        for c in loads:
            c.wait()
        def tile(o, hh, carry):
            t = 2 * o + hh

            def ahead(which):
                if o < NS // 2 - 1:
                    for c in fetch(which, o + hh, 1 - hh):
                        c.start()
                else:
                    @pl.when(hh == 0)
                    def _():
                        for c in fetch(which, o, 1):
                            c.start()

            for c in fetch(0, o, hh):
                c.wait()
            pre = jnp.dot(xs[0].reshape(rows, half), wcat[:half, :], preferred_element_type=F32)
            pre = pre + jnp.dot(xs[1].reshape(rows, half), wcat[half:, :], preferred_element_type=F32)
            ahead(0)
            for c in fetch(1, o, hh):
                c.wait()
            back = lax.dot_general(ds[0].reshape(rows, half), wdown[:, :half], NT, preferred_element_type=F32)
            back = back + lax.dot_general(ds[1].reshape(rows, half), wdown[:, half:], NT, preferred_element_type=F32)
            ahead(1)
            gate_pre, up_pre = pre[:, :LANE], pre[:, LANE:]
            scale = gates[t]
            sigma = jax.nn.sigmoid(gate_pre)
            silu = gate_pre * sigma
            act = silu * up_pre
            dact = scale * back
            grad_gate = dact * up_pre * sigma * (1.0 + gate_pre * (1.0 - sigma))
            grad_up = dact * silu
            cols = pl.ds(pl.multiple_of(t * rows, rows), rows)
            gt[:LANE, cols] = grad_gate.T.astype(BF16)
            gt[LANE:, cols] = grad_up.T.astype(BF16)
            wt[:, cols] = (scale * act).T.astype(BF16)
            sums = jnp.sum((act * back).T, axis=0, keepdims=True)
            for g in range(group):
                score[hh * group + g, :, o * ROWS:(o + 1) * ROWS] = sums[:, g * ROWS:(g + 1) * ROWS]
            both = jnp.concatenate([grad_gate.astype(BF16), grad_up.astype(BF16)], axis=1)
            for j in range(torus.nzl * n["x"]):
                zl, x = j // n["x"], j % n["x"]
                grad = lax.dot_general(both, wcat[j * width:(j + 1) * width, :], NT, preferred_element_type=F32)
                grad = grad.reshape(hz, n["y"], 2, 2, OCT, width).astype(BF16)
                for k in range(2):
                    part[k, zl, pl.ds(hh * hz, hz), :, 2 * o:2 * o + 2, :, x * width:(x + 1) * width] = grad[:, :, k]
            cross(o, hh).start()
            if o > 0:
                @pl.when(hh == 0)
                def _():
                    begin(o - 1)
            return carry

        for o in range(NS // 2):
            lax.fori_loop(0, 2, functools.partial(tile, o), 0)
            if o > 0:
                begun.extend((2 * o - 2, 2 * o - 1))
            while todo and todo[0][1] in begun and todo[0][0] < 12.0 * (o + 1) + 1.0:
                handle(todo.pop(0))

    pl.run_scoped(
        rows_phase,
        pltpu.VMEM((2, hz, n["y"], 2, ROWS, half), BF16), pltpu.VMEM((2, hz, n["y"], 2, ROWS, half), BF16),
        pltpu.SemaphoreType.DMA((2,)), pltpu.SemaphoreType.DMA((2,)))

    def message(q, offset, sign):
        p, k = torus.other_expert(pos, core, offset, sign)
        other = torus.device(p, k)
        return remote(score.at[other["exp"]], score_in.at[me if sign > 0 else other["exp"]],
                      s_send.at[q], s_recv.at[q], other)

    def share(q, offset, sign):
        to = torus.peer(pos, core, offset, sign)
        slot = my_et if sign > 0 else to["et"]
        return remote(score_in, score_all.at[slot], h_send.at[q], h_recv.at[q], to)

    def hand(q, offset, sign):
        to = torus.peer(pos, core, offset, sign)
        slot = my_et if sign > 0 else to["et"]
        return remote(ship.at[to["et"]], inbox.at[slot], e_send.at[q], e_recv.at[q], to)

    for q, offset in enumerate(torus.experts()):
        message(q, offset, 1).start()
    score_in[me] = score[me]

    def exchange(xt, dt, sg, su, sd, x_sem, d_sem, o_sem):
        units = depth // tile_cols
        per = half // tile_cols

        def fetch(u, which):
            buf, sem = (xt, x_sem) if which == 0 else (dt, d_sem)
            d, c = u // per, pl.ds(u % per * tile_cols, tile_cols)
            return [pltpu.make_async_copy(every.at[which, d, pl.ds(t % 2 * hz, hz), :, :, t // 2, :, c],
                                          buf.at[u % 2, t], sem.at[u % 2, t]) for t in range(tiles)]

        def put(u):
            c = pl.ds(u * tile_cols, tile_cols)
            return [pltpu.make_async_copy(sg.at[u % 2], dg.at[c], o_sem.at[u % 2, 0]),
                    pltpu.make_async_copy(su.at[u % 2], du.at[c], o_sem.at[u % 2, 1]),
                    pltpu.make_async_copy(sd.at[u % 2], dd.at[:, c], o_sem.at[u % 2, 2])]

        def get(u):
            for which in range(2):
                for c in fetch(u, which):
                    c.start()

        def unit(u):
            if u + 1 < units:
                get(u + 1)
            for which in range(2):
                for c in fetch(u, which):
                    c.wait()
            if u >= 2:
                for c in put(u - 2):
                    c.wait()
            both = jnp.dot(gt[...], xt[u % 2].reshape(tiles * rows, tile_cols), preferred_element_type=F32).T
            sg[u % 2] = both[:, :LANE].astype(BF16)
            su[u % 2] = both[:, LANE:].astype(BF16)
            down = jnp.dot(wt[...], dt[u % 2].reshape(tiles * rows, tile_cols), preferred_element_type=F32)
            sd[u % 2] = down.astype(BF16)
            for c in put(u):
                c.start()

        get(0)
        begin(2)
        total = len(todo)
        done = 0
        for i, event in enumerate(todo):
            if i == 4:
                for q, offset in enumerate(torus.experts()):
                    message(q, offset, -1).wait_recv()
                for q, offset in enumerate(torus.peers()):
                    share(q, offset, 1).start()
                score_all[my_et] = score_in[...]
            while done < units - 2 and done * total * 3 // 5 <= i * (units - 2):
                unit(done)
                done += 1
            handle(event)
        count = out.shape[1]
        for i in range(out.shape[0]):
            ship[i] = fin[i * count:(i + 1) * count, :].astype(BF16)
        for q, offset in enumerate(torus.peers()):
            hand(q, offset, 1).start()
        inbox[my_et] = ship[my_et]
        while done < units:
            unit(done)
            done += 1
        for u in (units - 2, units - 1):
            for c in put(u):
                c.wait()

    stage = pltpu.VMEM((2, tile_cols, LANE), BF16)
    tiled = pltpu.VMEM((2, tiles, hz, n["y"], 2, ROWS, tile_cols), BF16)
    dma = pltpu.SemaphoreType.DMA
    pl.run_scoped(exchange, tiled, tiled, stage, stage, pltpu.VMEM((2, LANE, tile_cols), BF16),
                  dma((2, tiles)), dma((2, tiles)), dma((2, 3)))

    for q, offset in enumerate(torus.peers()):
        hand(q, offset, -1).wait_recv()
        share(q, offset, -1).wait_recv()
    out[...] = inbox[...]
    score_out[...] = score_all[...]
    for q, offset in enumerate(torus.peers()):
        hand(q, offset, 1).wait_send()
        share(q, offset, 1).wait_send()
    for q, offset in enumerate(torus.experts()):
        message(q, offset, 1).wait_send()
    for t in range(tiles):
        cross(t // 2, t % 2).wait_send()
    for s in range(NS):
        order = BACK[s // 2]
        for phase in (0, 1):
            for k in range(n[order[phase]] - 1):
                for q in range(n[order[1]] if phase == 0 else 1):
                    ring(s, phase, k, q).wait_send()
        for by in range(1, n[order[2]]):
            last(s, by).wait_send()


def back_all(torus, every, gates, wg, wu, wd):
    n = torus.n
    depth = wg.shape[0]
    width = depth // (torus.nzl * n["x"])
    wide = n["x"] * width
    experts = torus.nzh * n["y"] * 2
    bufs = []
    for order in BACK:
        for phase, axis in enumerate(order):
            free = order[2:] if phase < 2 else ()
            shape = (2, n[axis] - 1)
            if phase == 0:
                shape += (n[order[1]],)
            if "z" in free:
                shape += (torus.nzl, torus.nzh)
            if "y" in free:
                shape += (n["y"],)
            shape += (OCT, wide if "x" in free else width)
            bufs.append(pltpu.VMEM(shape, BF16))
    most = max(n.values()) - 1
    others, peers = len(torus.experts()), len(torus.peers())
    n_et = peers + 1
    total = experts * NS * OCT
    owned = (n_et, NS * OCT // n_et, width)
    dma = pltpu.SemaphoreType.DMA
    vm = pltpu.VMEM
    half = (torus.nzl, torus.nzh, n["y"], NS, OCT, wide)
    any_ = pl.BlockSpec(memory_space=pl.ANY)
    vspec = pl.BlockSpec(memory_space=pltpu.VMEM)
    return pl.pallas_call(
        functools.partial(back_kernel, torus, depth, min(512, depth // 2)),
        out_shape=[jax.ShapeDtypeStruct(owned, BF16),
                   jax.ShapeDtypeStruct((n_et, experts, 1, LANE), F32),
                   jax.ShapeDtypeStruct((depth, LANE), BF16),
                   jax.ShapeDtypeStruct((depth, LANE), BF16),
                   jax.ShapeDtypeStruct((LANE, depth), BF16)],
        in_specs=[any_, vspec, any_, any_, any_],
        out_specs=[vspec, vspec, any_, any_, any_],
        scratch_shapes=[vm((2,) + half, BF16), vm(half, BF16), vm((depth, 2 * LANE), BF16), vm((LANE, depth), BF16),
                        vm((2 * LANE, total), BF16), vm((LANE, total), BF16), vm((experts, 1, LANE), F32),
                        vm((experts, 1, LANE), F32), vm((n_et, experts, 1, LANE), F32), vm((NS * OCT, width), F32),
                        vm(owned, BF16), vm(owned, BF16), *bufs, dma((3,)), dma((NS,)), dma((NS,)),
                        dma((NS, 2, most, 4)), dma((NS, 2, most, 4)), dma((NS, most)), dma((NS, most)),
                        dma((others,)), dma((others,)), dma((peers,)), dma((peers,)), dma((peers,)), dma((peers,))],
        compiler_params=pltpu.CompilerParams(
            collective_id=1, has_side_effects=True, vmem_limit_bytes=67043328),
        name="back_all",
    )(every, gates, wg, wu, wd)


def on_device(torus, tokens, grad_out, gates, expert_ids, gate_weight, up_weight, down_weight):
    count, depth = tokens.shape
    n = torus.n
    n_et = torus.nzl * n["x"]
    n_exp = torus.nzh * n["y"] * 2
    share = depth // (2 * n["x"])
    experts = jnp.arange(LANE, dtype=jnp.int32)
    chosen = expert_ids[:, :, None] == experts[None, None, :]
    table = jnp.sum(jnp.where(chosen, gates[:, :, None].astype(F32), 0.0), axis=1).astype(BF16)
    both = jnp.stack([tokens, grad_out], axis=0).reshape(2, count, 2, n["x"], share)
    packed = both.transpose(0, 3, 1, 2, 4).reshape(n_et, count, 2 * share)
    sel = jnp.pad(table.astype(F32).T[:n_exp], ((0, 0), (0, LANE - count)))[:, None, :]
    every, scale = gather_all(torus, packed, sel)
    rows = n_et * count
    scale = scale[:, :, 0, :count].transpose(1, 0, 2).reshape(2, n_exp // 2, NS // 2, ROWS).transpose(2, 0, 1, 3)
    scale = jnp.broadcast_to(scale.reshape(NS, n_exp // 2 * ROWS, 1), (NS, n_exp // 2 * ROWS, LANE))
    owned, score, dg, du, dd = back_all(torus, every, scale, gate_weight[0], up_weight[0], down_weight[0])
    input_grad = owned.transpose(1, 0, 2).reshape(count, depth)
    score = score[:, :, 0, :rows].reshape(n_et, n_exp, n_et, count)
    score = lax.dynamic_index_in_dim(score, lax.axis_index("et"), axis=2, keepdims=False)
    score = jnp.sum(score.astype(BF16).astype(F32), axis=0)
    chosen = chosen[:, :, :n_exp]
    gate_grad = jnp.sum(jnp.where(chosen, score.T[:, None, :], 0.0), axis=2)
    return input_grad, gate_grad, dg[None], du[None], dd[None]


def solution(mesh, dims=(4, 4, 4, 2)):
    placed = (
        P(("exp", "et"), None),
        P(("exp", "et"), None),
        P(("exp", "et"), None),
        P(("exp", "et"), None),
        P("exp", None, "et"),
        P("exp", None, "et"),
        P("exp", "et", None),
    )
    return jax.shard_map(
        functools.partial(on_device, Torus(*dims)),
        mesh=mesh,
        in_specs=placed,
        out_specs=(
            P(("exp", "et"), None),
            P(("exp", "et"), None),
            P("exp", None, "et"),
            P("exp", None, "et"),
            P("exp", "et", None),
        ),
        check_vma=False,
    )
```

```python
import functools
import jax
import jax.numpy as jnp
from jax import lax
from jax.experimental import pallas as pl
from jax.experimental.pallas import tpu as pltpu
from jax.sharding import PartitionSpec as P

TOP = 8
LANE = 128
NS = 6
OCT = 8
MESH = pl.DeviceIdType.MESH
ORDERS = (("x", "y", "z"), ("z", "y", "x"), ("z", "x", "y"))
ROWS = 16
NT = (((1,), (1,)), ((), ()))
F32 = jnp.float32
BF16 = jnp.bfloat16


class Torus:
    def __init__(self, nx, ny, nzh, nzl):
        self.n = {"x": nx, "y": ny, "z": nzh * nzl}
        self.nzh, self.nzl = nzh, nzl

    def here(self):
        e = lax.axis_index("exp")
        t = lax.axis_index("et")
        ny, nx = self.n["y"], self.n["x"]
        core = lax.rem(e, 2)
        y = lax.rem(lax.div(e, 2), ny)
        zh = lax.div(e, 2 * ny)
        x = lax.rem(t, nx)
        zl = lax.div(t, nx)
        return {"x": x, "y": y, "z": zh * self.nzl + zl}, core

    def split(self, z):
        return lax.rem(z, self.nzl), lax.div(z, self.nzl)

    def device(self, pos, core):
        zl, zh = self.split(pos["z"])
        return {
            "exp": (zh * self.n["y"] + pos["y"]) * 2 + core,
            "et": zl * self.n["x"] + pos["x"],
        }

    def shift(self, pos, axis, by):
        n = self.n[axis]
        return lax.rem(pos[axis] + (by % n + n), n)

    def moved(self, pos, axis, by):
        other = dict(pos)
        other[axis] = self.shift(pos, axis, by)
        return other

    def experts(self):
        return [(c, y, h) for c in range(2) for y in range(self.n["y"]) for h in range(self.nzh) if c or y or h]

    def other_expert(self, pos, core, offset, sign):
        c, y, h = offset
        out = self.moved(pos, "y", sign * y)
        out["z"] = self.shift(pos, "z", sign * h * self.nzl)
        return out, (1 - core if c else core)

    def peers(self):
        return [(l, x) for l in range(self.nzl) for x in range(self.n["x"]) if l or x]

    def peer(self, pos, core, offset, sign):
        l, x = offset
        out = self.moved(pos, "x", sign * x)
        zl, zh = self.split(pos["z"])
        out["z"] = zh * self.nzl + (lax.rem(zl + l, self.nzl) if l else zl)
        return self.device(out, core)

    def greet(self, pos, core):
        seen, partners = set(), []
        for c, y, h in self.experts():
            p, k = self.other_expert(pos, core, (c, y, h), 1)
            partners.append(self.device(p, k))
            if not c and not y:
                seen.add(("z", h * self.nzl))
            if not c and not h:
                seen.add(("y", y))
        for axis in "xyz":
            for by in range(1, self.n[axis]):
                if (axis, by) not in seen:
                    partners.append(self.device(self.moved(pos, axis, by), core))
        for l, x in self.peers():
            if l and x:
                partners.append(self.peer(pos, core, (l, x), 1))
        barrier = pltpu.get_barrier_semaphore()
        for p in partners:
            pl.semaphore_signal(barrier, inc=1, device_id=p, device_id_type=MESH)
        pl.semaphore_wait(barrier, len(partners))


def remote(src, dst, send, recv, device):
    return pltpu.make_async_remote_copy(
        src_ref=src, dst_ref=dst, send_sem=send, recv_sem=recv, device_id=device, device_id_type=MESH)


def chosen_part(torus, at, part, width):
    zl, zh, y = slice(None), slice(None), slice(None)
    if at["z"] is not None:
        zl, zh = torus.split(at["z"])
    if at["y"] is not None:
        y = at["y"]
    col = slice(None)
    if at["x"] is not None:
        col = pl.ds(pl.multiple_of(at["x"] * width, LANE), width)
    if part is not None:
        if at["z"] is None:
            zl = part
        elif at["y"] is None:
            n = torus.n["y"] // 2
            y = pl.ds(part * n, n)
        else:
            n = torus.n["x"] // 2 * width
            col = pl.ds(part * n, n)
    return zl, zh, y, col


def volume(torus, axes):
    w = 1
    for a in axes:
        w *= torus.n[a]
    return w


def gather_kernel(torus, width, packed, sel, out, gate_out, gate_in, gate_all, inbox, stack, blk, loc, p1_send, p1_recv,
                  send, recv, sib_send, sib_recv, g_send, g_recv, e_send, e_recv, h_send, h_recv):
    pos, core = torus.here()
    me = torus.device(pos, core)["exp"]
    my_et = torus.device(pos, core)["et"]
    sibling = torus.device(pos, 1 - core)
    torus.greet(pos, core)

    def hand(q, offset, sign):
        to = torus.peer(pos, core, offset, sign)
        slot = my_et if sign > 0 else to["et"]
        return remote(packed.at[to["et"]], inbox.at[slot], e_send.at[q], e_recv.at[q], to)

    def share(q, offset, sign):
        to = torus.peer(pos, core, offset, sign)
        slot = my_et if sign > 0 else to["et"]
        return remote(gate_in, gate_all.at[slot], h_send.at[q], h_recv.at[q], to)

    for q, offset in enumerate(torus.peers()):
        hand(q, offset, 1).start()
    for q, offset in enumerate(torus.experts()):
        p, k = torus.other_expert(pos, core, offset, 1)
        to = torus.device(p, k)
        remote(sel.at[to["exp"]], gate_in.at[me], g_send.at[q], g_recv.at[q], to).start()
    gate_in[me] = sel[me]
    inbox[my_et] = packed[my_et]
    for q, offset in enumerate(torus.peers()):
        hand(q, offset, -1).wait_recv()
    count = packed.shape[1]
    for i in range(packed.shape[0]):
        stack[i * count:(i + 1) * count, :] = inbox[i].astype(F32)
    for d in range(2):
        for o in range(NS // 2):
            blk[d, o] = stack[o * ROWS:(o + 1) * ROWS, d * width:(d + 1) * width].astype(BF16)

    def region(s, phase, shift, part=None, c=core):
        order = ORDERS[s // 2]
        at = dict(pos)
        for axis in order[:phase]:
            at[axis] = None
        if phase < 3:
            at[order[phase]] = torus.shift(pos, order[phase], shift)
        zl, zh, y, col = chosen_part(torus, at, part, width)
        return out.at[zl, s % 2, zh, y, c, s // 2, :, col]

    def reach(s):
        n = torus.n[ORDERS[s // 2][0]]
        up = n // 2 if s % 2 == 0 else n - 1 - n // 2
        return up, n - 1 - up

    def first(s, d, hop):
        i = hop - 1 if d > 0 else reach(s)[0] + hop - 1
        here = region(s, 0, -d * (hop - 1))
        src = blk.at[s % 2, s // 2] if hop == 1 else here
        return remote(src, here, p1_send.at[s, i], p1_recv.at[s, i],
                      torus.device(torus.moved(pos, ORDERS[s // 2][0], d), core))

    def first_landed(s, d, hop):
        i = hop - 1 if d > 0 else reach(s)[0] + hop - 1
        here = region(s, 0, -d * hop)
        return remote(here, here, p1_send.at[s, i], p1_recv.at[s, i], sibling)

    def chain(s):
        up, down = reach(s)
        return [(d, h) for h in range(1, max(up, down) + 1) for d in (1, -1) if h <= (up if d > 0 else down)]

    def ring(s, phase, k, part):
        d = 1 if s % 2 == 0 else -1
        here = region(s, phase, -d * k, part)
        i = phase - 1
        return remote(here, here, send.at[s, i, k, part], recv.at[s, i, k, part],
                      torus.device(torus.moved(pos, ORDERS[s // 2][phase], d), core))

    def landed(s, phase, k, part):
        d = 1 if s % 2 == 0 else -1
        here = region(s, phase, -d * (k + 1), part)
        return remote(here, here, send.at[s, phase - 1, k, part], recv.at[s, phase - 1, k, part], sibling)

    def across(s, src, dst):
        return remote(src, dst, sib_send.at[s], sib_recv.at[s], sibling)

    def own(s):
        return pltpu.make_async_copy(blk.at[s % 2, s // 2], region(s, 0, 0), loc.at[s])

    for s in range(NS):
        for d, h in chain(s):
            if h == 1:
                first(s, d, 1).start()
        own(s).start()
    for s in range(NS):
        own(s).wait()
    for hop in range(1, max(torus.n.values()) // 2 + 1):
        for s in range(NS):
            mine = [(d, h) for d, h in chain(s) if h == hop]
            for d, h in mine:
                first_landed(s, d, h).wait_recv()
                if (d, h + 1) in chain(s):
                    first(s, d, h + 1).start()
            if mine and hop == max(h for _, h in chain(s)):
                for part in range(2):
                    ring(s, 1, 0, part).start()
                whole = region(s, 1, 0)
                across(s, whole, whole).start()
    for q, offset in enumerate(torus.experts()):
        p, k = torus.other_expert(pos, core, offset, -1)
        came = torus.device(p, k)
        remote(sel.at[me], gate_in.at[came["exp"]], g_send.at[q], g_recv.at[q], came).wait_recv()
    for q, offset in enumerate(torus.peers()):
        share(q, offset, 1).start()
    gate_all[my_et] = gate_in[...]
    events = []
    for s in range(NS):
        order = ORDERS[s // 2]
        at = 20.0 if order[0] == "x" else 30.0
        for phase in (1, 2):
            w = volume(torus, order[:phase]) * 0.66
            for k in range(torus.n[order[phase]] - 1):
                for part in range(2):
                    at += w / 2 + (0.8 if phase == 1 else 0.3)
                    events.append((at, s, phase, k, part))
            at += 1.5
    for _, s, phase, k, part in sorted(events):
        order = ORDERS[s // 2]
        arrived = landed(s, phase, k, part)
        arrived.wait_recv()
        if k + 1 < torus.n[order[phase]] - 1:
            ring(s, phase, k + 1, part).start()
        elif phase == 1 and part == 1:
            for half in range(2):
                ring(s, 2, 0, half).start()
        d = 1 if s % 2 == 0 else -1
        here = region(s, phase, -d * (k + 1), part)
        across(s, here, here).start()
    for q, offset in enumerate(torus.peers()):
        share(q, offset, -1).wait_recv()
    gate_out[...] = gate_all[...]
    for q, offset in enumerate(torus.peers()):
        share(q, offset, 1).wait_send()
        hand(q, offset, 1).wait_send()
    for s in range(NS):
        order = ORDERS[s // 2]
        for d, h in chain(s):
            first(s, d, h).wait_send()
        for phase in (1, 2):
            for k in range(torus.n[order[phase]] - 1):
                for part in range(2):
                    ring(s, phase, k, part).wait_send()
        whole, other = region(s, 3, 0), region(s, 3, 0, None, 1 - core)
        across(s, whole, whole).wait_send()
        across(s, other, other).wait_recv()
    for q, offset in enumerate(torus.experts()):
        p, k = torus.other_expert(pos, core, offset, 1)
        to = torus.device(p, k)
        remote(sel.at[to["exp"]], gate_in.at[me], g_send.at[q], g_recv.at[q], to).wait_send()


def gather_all(torus, packed, sel):
    width = packed.shape[2] // 2
    n = torus.n
    shape = (torus.nzl, 2, torus.nzh, n["y"], 2, NS // 2, ROWS, n["x"] * width)
    most = max(n.values()) - 1
    others, peers = len(torus.experts()), len(torus.peers())
    gates = (packed.shape[0],) + sel.shape
    dma = pltpu.SemaphoreType.DMA
    vm = pltpu.VMEM
    return pl.pallas_call(
        functools.partial(gather_kernel, torus, width),
        out_shape=[jax.ShapeDtypeStruct(shape, packed.dtype), jax.ShapeDtypeStruct(gates, sel.dtype)],
        in_specs=[pl.BlockSpec(memory_space=pltpu.VMEM)] * 2,
        out_specs=[pl.BlockSpec(memory_space=pl.ANY), pl.BlockSpec(memory_space=pltpu.VMEM)],
        scratch_shapes=[vm(sel.shape, sel.dtype), vm(gates, sel.dtype), vm(packed.shape, packed.dtype),
                        vm((NS * OCT, 2 * width), F32), vm((2, NS // 2, ROWS, width), packed.dtype),
                        dma((NS,)), dma((NS, most)), dma((NS, most)),
                        dma((NS, 2, most, 2)), dma((NS, 2, most, 2)), dma((NS,)), dma((NS,)),
                        dma((others,)), dma((others,)), dma((peers,)), dma((peers,)), dma((peers,)), dma((peers,))],
        compiler_params=pltpu.CompilerParams(collective_id=0, has_side_effects=True),
        name="gather_all",
    )(packed, sel)


BACK = tuple(tuple(reversed(o)) for o in ORDERS)


def back_kernel(torus, depth, tile_cols, every, gates, wg, wu, wd, out, score_out, dg, du, dd,
                part, theirs, wcat, wdown, gt, wt, score, score_in, score_all, fin, ship, inbox, b0, b1, b2, b3, b4, b5, b6, b7, b8,
                w_sem, sib_send, sib_recv, send, recv, p3_send, p3_recv, s_send, s_recv, e_send, e_recv, h_send, h_recv):
    bufs = (b0, b1, b2, b3, b4, b5, b6, b7, b8)
    n = torus.n
    width = depth // (torus.nzl * n["x"])
    wide = n["x"] * width
    pos, core = torus.here()
    me = torus.device(pos, core)["exp"]
    my_et = torus.device(pos, core)["et"]
    sibling = torus.device(pos, 1 - core)
    hz = torus.nzh // 2
    group = hz * n["y"] * 2
    rows = group * ROWS
    tiles = NS
    half = depth // 2

    loads = [pltpu.make_async_copy(wg, wcat.at[:, pl.ds(0, LANE)], w_sem.at[0]),
             pltpu.make_async_copy(wu, wcat.at[:, pl.ds(LANE, LANE)], w_sem.at[1]),
             pltpu.make_async_copy(wd, wdown, w_sem.at[2])]
    for c in loads:
        c.start()

    def block(at, s, k=core):
        zl, zh, y, col = chosen_part(torus, at, None, width)
        return part.at[k, zl, zh, y, s, :, col]

    def place(s, phase, shift):
        order = BACK[s // 2]
        at = dict(pos)
        for axis in order[phase + 1:]:
            at[axis] = None
        at[order[phase]] = torus.shift(pos, order[phase], shift)
        return at

    def piece(at, s, h):
        zl, zh, y, col = chosen_part(torus, at, h, width)
        return part.at[core, zl, zh, y, s, :, col]

    def slot(s, phase, k, h):
        ref = bufs[s // 2 * 3 + phase].at[s % 2, k]
        if h is None:
            return ref
        order = BACK[s // 2]
        if "z" in order[phase + 1:]:
            return ref.at[h]
        if "y" in order[phase + 1:]:
            return ref.at[pl.ds(h * (n["y"] // 2), n["y"] // 2)]
        return ref.at[:, pl.ds(h * (n["x"] // 2) * width, n["x"] // 2 * width)]

    def ring(s, phase, k, h):
        d = 1 if s % 2 == 0 else -1
        return remote(piece(place(s, phase, -d * (k + 1)), s, h), slot(s, phase, k, h),
                      send.at[s, phase, k, h], recv.at[s, phase, k, h],
                      torus.device(torus.moved(pos, BACK[s // 2][phase], d), core))

    def last(s, by):
        axis = BACK[s // 2][2]
        return remote(block(place(s, 2, by), s), bufs[s // 2 * 3 + 2].at[s % 2, by - 1],
                      p3_send.at[s, by - 1], p3_recv.at[s, by - 1],
                      torus.device(torus.moved(pos, axis, by), core))

    def add(s, at, got, h):
        zl0, zh0, y0, col0 = None, None, None, None
        nzl, nzh, ny = 1, 1, 1
        zbase = ybase = 0
        if at["z"] is None:
            nzh = torus.nzh
            nzl = torus.nzl if h is None else 1
            zbase = 0 if h is None else h
        else:
            zl0, zh0 = torus.split(at["z"])
        if at["y"] is None:
            ny = n["y"]
            if h is not None and at["z"] is not None:
                ny, ybase = n["y"] // 2, h * (n["y"] // 2)
        else:
            y0 = at["y"]
        if at["x"] is None:
            cols = wide
            col0 = pl.ds(0, wide)
            if h is not None and at["z"] is not None and at["y"] is not None:
                cols = wide // 2
                col0 = pl.ds(h * cols, cols)
        else:
            cols = width
            col0 = pl.ds(pl.multiple_of(at["x"] * width, LANE), width)

        def one(i, carry):
            iy = lax.rem(i, ny)
            iz = lax.div(i, ny)
            izh = lax.rem(iz, nzh)
            izl = lax.div(iz, nzh)
            where = ()
            if at["z"] is None:
                where = (izh,) if h is not None else (izl, izh)
                zl, zh = izl + zbase, izh
            else:
                zl, zh = zl0, zh0
            if at["y"] is None:
                where = where + (iy,)
                y = iy + ybase
            else:
                y = y0
            part[core, zl, zh, y, s, :, col0] += got[where + (slice(None), slice(None))]
            return carry

        lax.fori_loop(0, nzl * nzh * ny, one, 0)

    def cross(t):
        o, hh = t // 2, t % 2
        zs, os = pl.ds(hh * hz, hz), pl.ds(2 * o, 2)
        return remote(part.at[1 - core, :, zs, :, os], theirs.at[:, zs, :, os], sib_send.at[t], sib_recv.at[t], sibling)

    everywhere = {"x": None, "y": None, "z": None}

    def begin(o):
        for t in (2 * o, 2 * o + 1):
            cross(t).wait_recv()
        for s in (2 * o, 2 * o + 1):
            add(s, everywhere, theirs.at[:, :, :, s], None)
            for h in range(2):
                ring(s, 0, 0, h).start()

    def rows_phase(xs, ds, x_sem, d_sem):
        def fetch(which, t):
            o, hh = t // 2, t % 2
            buf, sem = (xs, x_sem) if which == 0 else (ds, d_sem)
            return [pltpu.make_async_copy(every.at[which, d, pl.ds(hh * hz, hz), :, :, o], buf.at[d], sem.at[d])
                    for d in range(2)]

        for which in range(2):
            for c in fetch(which, 0):
                c.start()
        score[...] = jnp.zeros_like(score)
        torus.greet(pos, core)
        for c in loads:
            c.wait()
        for t in range(tiles):
            o, hh = t // 2, t % 2
            for c in fetch(0, t):
                c.wait()
            pre = jnp.dot(xs[0].reshape(rows, half), wcat[:half, :], preferred_element_type=F32)
            pre = pre + jnp.dot(xs[1].reshape(rows, half), wcat[half:, :], preferred_element_type=F32)
            if t + 1 < tiles:
                for c in fetch(0, t + 1):
                    c.start()
            for c in fetch(1, t):
                c.wait()
            back = lax.dot_general(ds[0].reshape(rows, half), wdown[:, :half], NT, preferred_element_type=F32)
            back = back + lax.dot_general(ds[1].reshape(rows, half), wdown[:, half:], NT, preferred_element_type=F32)
            if t + 1 < tiles:
                for c in fetch(1, t + 1):
                    c.start()
            gate_pre, up_pre = pre[:, :LANE], pre[:, LANE:]
            scale = gates[t]
            sigma = jax.nn.sigmoid(gate_pre)
            silu = gate_pre * sigma
            act = silu * up_pre
            dact = scale * back
            grad_gate = dact * up_pre * sigma * (1.0 + gate_pre * (1.0 - sigma))
            grad_up = dact * silu
            cols = pl.ds(t * rows, rows)
            gt[:LANE, cols] = grad_gate.T.astype(BF16)
            gt[LANE:, cols] = grad_up.T.astype(BF16)
            wt[:, cols] = (scale * act).T.astype(BF16)
            sums = jnp.sum((act * back).T, axis=0, keepdims=True)
            for g in range(group):
                score[hh * group + g, :, o * ROWS:(o + 1) * ROWS] = sums[:, g * ROWS:(g + 1) * ROWS]
            both = jnp.concatenate([grad_gate.astype(BF16), grad_up.astype(BF16)], axis=1)
            for j in range(torus.nzl * n["x"]):
                zl, x = j // n["x"], j % n["x"]
                grad = lax.dot_general(both, wcat[j * width:(j + 1) * width, :], NT, preferred_element_type=F32)
                grad = grad.reshape(hz, n["y"], 2, 2, OCT, width).astype(BF16)
                for k in range(2):
                    part[k, zl, hh * hz:(hh + 1) * hz, :, 2 * o:2 * o + 2, :, x * width:(x + 1) * width] = grad[:, :, k]
            cross(t).start()
            if t in (2, 4):
                begin(t // 2 - 1)

    pl.run_scoped(
        rows_phase,
        pltpu.VMEM((2, hz, n["y"], 2, ROWS, half), BF16), pltpu.VMEM((2, hz, n["y"], 2, ROWS, half), BF16),
        pltpu.SemaphoreType.DMA((2,)), pltpu.SemaphoreType.DMA((2,)))

    def message(q, offset, sign):
        p, k = torus.other_expert(pos, core, offset, sign)
        other = torus.device(p, k)
        return remote(score.at[other["exp"]], score_in.at[me if sign > 0 else other["exp"]],
                      s_send.at[q], s_recv.at[q], other)

    def share(q, offset, sign):
        to = torus.peer(pos, core, offset, sign)
        slot = my_et if sign > 0 else to["et"]
        return remote(score_in, score_all.at[slot], h_send.at[q], h_recv.at[q], to)

    def hand(q, offset, sign):
        to = torus.peer(pos, core, offset, sign)
        slot = my_et if sign > 0 else to["et"]
        return remote(ship.at[to["et"]], inbox.at[slot], e_send.at[q], e_recv.at[q], to)

    for q, offset in enumerate(torus.experts()):
        message(q, offset, 1).start()
    score_in[me] = score[me]

    def exchange(xt, dt, sg, su, sd, x_sem, d_sem, o_sem):
        units = depth // tile_cols
        per = half // tile_cols

        def fetch(u, which):
            buf, sem = (xt, x_sem) if which == 0 else (dt, d_sem)
            d, c = u // per, pl.ds(u % per * tile_cols, tile_cols)
            return [pltpu.make_async_copy(every.at[which, d, pl.ds(t % 2 * hz, hz), :, :, t // 2, :, c],
                                          buf.at[u % 2, t], sem.at[u % 2, t]) for t in range(tiles)]

        def put(u):
            c = pl.ds(u * tile_cols, tile_cols)
            return [pltpu.make_async_copy(sg.at[u % 2], dg.at[c], o_sem.at[u % 2, 0]),
                    pltpu.make_async_copy(su.at[u % 2], du.at[c], o_sem.at[u % 2, 1]),
                    pltpu.make_async_copy(sd.at[u % 2], dd.at[:, c], o_sem.at[u % 2, 2])]

        def get(u):
            for which in range(2):
                for c in fetch(u, which):
                    c.start()

        def unit(u):
            if u + 1 < units:
                get(u + 1)
            for which in range(2):
                for c in fetch(u, which):
                    c.wait()
            if u >= 2:
                for c in put(u - 2):
                    c.wait()
            both = jnp.dot(gt[...], xt[u % 2].reshape(tiles * rows, tile_cols), preferred_element_type=F32).T
            sg[u % 2] = both[:, :LANE].astype(BF16)
            su[u % 2] = both[:, LANE:].astype(BF16)
            down = jnp.dot(wt[...], dt[u % 2].reshape(tiles * rows, tile_cols), preferred_element_type=F32)
            sd[u % 2] = down.astype(BF16)
            for c in put(u):
                c.start()

        get(0)
        events = []
        for s in range(NS):
            order = BACK[s // 2]
            at = (0.0, 5.0, 12.0)[s // 2]
            for phase in (0, 1):
                w = volume(torus, order[phase + 1:])
                for k in range(n[order[phase]] - 1):
                    for h in range(2):
                        at += w / 2 + 0.5
                        events.append((at, s, phase, k, h))
                at += 2.0
            events.append((at + 6.0, s, 2, 0, 0))
        events.sort()
        done = 0
        for i, (_, s, phase, k, h) in enumerate(events):
            if i == 4:
                begin(2)
                for q, offset in enumerate(torus.experts()):
                    message(q, offset, -1).wait_recv()
                for q, offset in enumerate(torus.peers()):
                    share(q, offset, 1).start()
                score_all[my_et] = score_in[...]
            while i >= 4 and done < units - 2 and done * len(events) * 3 // 5 <= i * (units - 2):
                unit(done)
                done += 1
            order = BACK[s // 2]
            d = 1 if s % 2 == 0 else -1
            if phase < 2:
                ring(s, phase, k, h).wait_recv()
                add(s, place(s, phase, -d * (k + 2)), slot(s, phase, k, h), h)
                if k + 1 < n[order[phase]] - 1:
                    ring(s, phase, k + 1, h).start()
                elif h == 1 and phase == 0:
                    for hh in range(2):
                        ring(s, 1, 0, hh).start()
                elif h == 1:
                    for by in range(1, n[order[2]]):
                        last(s, by).start()
            else:
                zl, zh = torus.split(pos["z"])
                col = pl.ds(pl.multiple_of(pos["x"] * width, LANE), width)
                total = part[core, zl, zh, pos["y"], s, :, col].astype(F32)
                for by in range(1, n[order[2]]):
                    last(s, by).wait_recv()
                    total = total + bufs[s // 2 * 3 + 2][s % 2, by - 1].astype(F32)
                fin[s * OCT:(s + 1) * OCT, :] = total
        count = out.shape[1]
        for i in range(out.shape[0]):
            ship[i] = fin[i * count:(i + 1) * count, :].astype(BF16)
        for q, offset in enumerate(torus.peers()):
            hand(q, offset, 1).start()
        inbox[my_et] = ship[my_et]
        while done < units:
            unit(done)
            done += 1
        for u in (units - 2, units - 1):
            for c in put(u):
                c.wait()

    stage = pltpu.VMEM((2, tile_cols, LANE), BF16)
    tiled = pltpu.VMEM((2, tiles, hz, n["y"], 2, ROWS, tile_cols), BF16)
    dma = pltpu.SemaphoreType.DMA
    pl.run_scoped(exchange, tiled, tiled, stage, stage, pltpu.VMEM((2, LANE, tile_cols), BF16),
                  dma((2, tiles)), dma((2, tiles)), dma((2, 3)))

    for q, offset in enumerate(torus.peers()):
        hand(q, offset, -1).wait_recv()
        share(q, offset, -1).wait_recv()
    out[...] = inbox[...]
    score_out[...] = score_all[...]
    for q, offset in enumerate(torus.peers()):
        hand(q, offset, 1).wait_send()
        share(q, offset, 1).wait_send()
    for q, offset in enumerate(torus.experts()):
        message(q, offset, 1).wait_send()
    for t in range(tiles):
        cross(t).wait_send()
    for s in range(NS):
        order = BACK[s // 2]
        for phase in (0, 1):
            for k in range(n[order[phase]] - 1):
                for h in range(2):
                    ring(s, phase, k, h).wait_send()
        for by in range(1, n[order[2]]):
            last(s, by).wait_send()


def back_all(torus, every, gates, wg, wu, wd):
    n = torus.n
    depth = wg.shape[0]
    width = depth // (torus.nzl * n["x"])
    wide = n["x"] * width
    experts = torus.nzh * n["y"] * 2
    bufs = []
    for order in BACK:
        for phase, axis in enumerate(order):
            free = order[phase + 1:]
            shape = (2, n[axis] - 1)
            if "z" in free:
                shape += (torus.nzl, torus.nzh)
            if "y" in free:
                shape += (n["y"],)
            shape += (OCT, wide if "x" in free else width)
            bufs.append(pltpu.VMEM(shape, BF16))
    most = max(n.values()) - 1
    others, peers = len(torus.experts()), len(torus.peers())
    n_et = peers + 1
    total = experts * NS * OCT
    owned = (n_et, NS * OCT // n_et, width)
    dma = pltpu.SemaphoreType.DMA
    vm = pltpu.VMEM
    half = (torus.nzl, torus.nzh, n["y"], NS, OCT, wide)
    any_ = pl.BlockSpec(memory_space=pl.ANY)
    vspec = pl.BlockSpec(memory_space=pltpu.VMEM)
    return pl.pallas_call(
        functools.partial(back_kernel, torus, depth, min(512, depth // 2)),
        out_shape=[jax.ShapeDtypeStruct(owned, BF16),
                   jax.ShapeDtypeStruct((n_et, experts, 1, LANE), F32),
                   jax.ShapeDtypeStruct((depth, LANE), BF16),
                   jax.ShapeDtypeStruct((depth, LANE), BF16),
                   jax.ShapeDtypeStruct((LANE, depth), BF16)],
        in_specs=[any_, vspec, any_, any_, any_],
        out_specs=[vspec, vspec, any_, any_, any_],
        scratch_shapes=[vm((2,) + half, BF16), vm(half, BF16), vm((depth, 2 * LANE), BF16), vm((LANE, depth), BF16),
                        vm((2 * LANE, total), BF16), vm((LANE, total), BF16), vm((experts, 1, LANE), F32),
                        vm((experts, 1, LANE), F32), vm((n_et, experts, 1, LANE), F32), vm((NS * OCT, width), F32),
                        vm(owned, BF16), vm(owned, BF16), *bufs, dma((3,)), dma((NS,)), dma((NS,)),
                        dma((NS, 2, most, 2)), dma((NS, 2, most, 2)), dma((NS, most)), dma((NS, most)),
                        dma((others,)), dma((others,)), dma((peers,)), dma((peers,)), dma((peers,)), dma((peers,))],
        compiler_params=pltpu.CompilerParams(
            collective_id=1, has_side_effects=True, vmem_limit_bytes=67043328),
        name="back_all",
    )(every, gates, wg, wu, wd)


def on_device(torus, tokens, grad_out, gates, expert_ids, gate_weight, up_weight, down_weight):
    count, depth = tokens.shape
    n = torus.n
    n_et = torus.nzl * n["x"]
    n_exp = torus.nzh * n["y"] * 2
    share = depth // (2 * n["x"])
    experts = jnp.arange(LANE, dtype=jnp.int32)
    chosen = expert_ids[:, :, None] == experts[None, None, :]
    table = jnp.sum(jnp.where(chosen, gates[:, :, None].astype(F32), 0.0), axis=1).astype(BF16)
    both = jnp.stack([tokens, grad_out], axis=0).reshape(2, count, 2, n["x"], share)
    packed = both.transpose(0, 3, 1, 2, 4).reshape(n_et, count, 2 * share)
    sel = jnp.pad(table.astype(F32).T[:n_exp], ((0, 0), (0, LANE - count)))[:, None, :]
    every, scale = gather_all(torus, packed, sel)
    rows = n_et * count
    scale = scale[:, :, 0, :count].transpose(1, 0, 2).reshape(2, n_exp // 2, NS // 2, ROWS).transpose(2, 0, 1, 3)
    scale = jnp.broadcast_to(scale.reshape(NS, n_exp // 2 * ROWS, 1), (NS, n_exp // 2 * ROWS, LANE))
    owned, score, dg, du, dd = back_all(torus, every, scale, gate_weight[0], up_weight[0], down_weight[0])
    input_grad = owned.transpose(1, 0, 2).reshape(count, depth)
    score = score[:, :, 0, :rows].reshape(n_et, n_exp, n_et, count)
    score = lax.dynamic_index_in_dim(score, lax.axis_index("et"), axis=2, keepdims=False)
    score = jnp.sum(score.astype(BF16).astype(F32), axis=0)
    chosen = chosen[:, :, :n_exp]
    gate_grad = jnp.sum(jnp.where(chosen, score.T[:, None, :], 0.0), axis=2)
    return input_grad, gate_grad, dg[None], du[None], dd[None]


def solution(mesh, dims=(4, 4, 4, 2)):
    placed = (
        P(("exp", "et"), None),
        P(("exp", "et"), None),
        P(("exp", "et"), None),
        P(("exp", "et"), None),
        P("exp", None, "et"),
        P("exp", None, "et"),
        P("exp", "et", None),
    )
    return jax.shard_map(
        functools.partial(on_device, Torus(*dims)),
        mesh=mesh,
        in_specs=placed,
        out_specs=(
            P(("exp", "et"), None),
            P(("exp", "et"), None),
            P("exp", None, "et"),
            P("exp", None, "et"),
            P("exp", "et", None),
        ),
        check_vma=False,
    )
```
